128 devices in a mesh: pr: 16 (over z, x), pc: 8 (over y, core).
Axes of the slice: x: 4, y: 4, z: 4, core: 2. Of those that a mesh axis runs over, the one named last changes fastest.
Arguments:
- trailing: float32 [20480, 20480], P('pr', 'pc'), may hold values from -25 to 25, as said below
- v_panels: float32 [6, 32, 20480], P(None, None, ('pr', 'pc')), may hold values from -0.078125 to 0.078125
- t_panels: float32 [6, 32, 32], replicated, may hold values from -0.2 to 0.5, as said below
Outputs:
- updated: float32 [20480, 20480], P('pr', 'pc')
- w_panels: float32 [6, 32, 20480], P(None, None, ('pr', 'pc'))
The draws below stay inside these ranges and needn't reach their ends.
Inputs may be any that keep to these rules, and one draw needn't show every extreme that they name: trailing is exactly symmetric. `t_panels`: each panel's factor is upper triangular with diagonal entries of 0.25 to 0.5.
All inputs are finite; a program needn't handle non-finite values.
Results may differ from the reference program's by a relative error of at most 0.00013.
Values sent between devices are 32-bit elements; how exact they have to be, the bound alone decides.
A program may use at most 128 MiB of HBM per device.

```python
import jax
import jax.numpy as jnp
from jax import lax

N = 20480
K = 32
PANELS = 6


def draw_trailing(key, part):
    noise = jax.random.normal(key, (N, N), jnp.float32)
    return jnp.clip((noise + noise.T) * 0.7071, -6.0, 6.0)


def draw_t_panels(key, part):
    row_ids = lax.broadcasted_iota(jnp.int32, (PANELS, K, K), 1)
    col_ids = lax.broadcasted_iota(jnp.int32, (PANELS, K, K), 2)
    diagonal = jax.random.uniform(jax.random.fold_in(key, 1), (PANELS, K, K), jnp.float32, 0.25, 0.5)
    upper = jnp.clip(0.04 * jax.random.normal(jax.random.fold_in(key, 2), (PANELS, K, K), jnp.float32), -0.2, 0.2)
    return jnp.where(row_ids == col_ids, diagonal, jnp.where(col_ids > row_ids, upper, 0.0))


def levels(own_key, shape, shards, least, high):
    def one(axis_at, parts):
        heights = jax.random.uniform(jax.random.fold_in(jax.random.fold_in(own_key, 6), axis_at), (parts,), jnp.float32, least / len(shards), high / len(shards))
        return jnp.repeat(jnp.exp(heights), shape[axis_at] // parts).reshape((-1,) + (1,) * (len(shape) - axis_at - 1))

    loudness = one(*shards[0])
    for cut in shards[1:]:
        loudness = loudness * one(*cut)
    return loudness


def scatter_about(rng, dims, deviation, bound, split=(), dtype=jnp.bfloat16):
    values = jax.random.normal(rng, dims, jnp.float32) * deviation
    if len(split) > 0:
        values = levels(rng, dims, split, -0.22, 0.18) * values
    return jnp.clip(values, min=-bound, max=bound).astype(dtype)


def setup_inputs(seed: int = 0) -> dict:
    seeds = jax.random.split(jax.random.key(seed), 4)
    trailing = draw_trailing(jax.random.fold_in(seeds[3], 71), 0)
    v_panels = scatter_about(seeds[1], (PANELS, K, N), (N // 4) ** -0.5, 0.078125, ((2, 128),), jnp.float32)
    t_panels = draw_t_panels(jax.random.fold_in(seeds[3], 71), 0)
    return {"trailing": trailing, "v_panels": v_panels, "t_panels": t_panels}


def contract(left_side, right_side, left_dim, right_dim):
    return lax.dot_general(left_side, right_side, (((left_dim,), (right_dim,)), ((), ())), precision=lax.Precision.HIGHEST, preferred_element_type=jnp.float32)


def reference(trailing, v_panels, t_panels):
    matrix = trailing
    w_blocks = []
    for panel in range(PANELS):
        house = v_panels[panel]
        factor = t_panels[panel]
        products = contract(house, matrix, 1, 1)
        gram_block = contract(house, products, 1, 1)
        middle = contract(contract(factor, gram_block, 0, 0), factor, 1, 0)
        w_block = contract(factor, products, 0, 0) - 0.5 * contract(middle, house, 0, 0)
        left_side = jnp.concatenate([house, w_block], axis=0)
        right_side = jnp.concatenate([w_block, house], axis=0)
        matrix = matrix - contract(left_side, right_side, 0, 0)
        w_blocks.append(w_block)
    return matrix, jnp.stack(w_blocks)
```

```python
import jax
import jax.numpy as jnp
from jax import lax
from jax.sharding import PartitionSpec as P

HIGHEST = lax.Precision.HIGHEST


def contract(left_side, right_side, left_dim, right_dim, precision=HIGHEST):
    return lax.dot_general(
        left_side,
        right_side,
        (((left_dim,), (right_dim,)), ((), ())),
        precision=precision,
        preferred_element_type=jnp.float32,
    )


def small_coefficients(gram_y, gram_v, t_panels):
    panels, width, _ = t_panels.shape
    size = panels * width
    eye = jnp.eye(size, dtype=jnp.float32)
    zero = jnp.zeros((size, size), jnp.float32)
    of_y = jnp.concatenate([gram_y, zero, eye], axis=1)
    of_v = jnp.concatenate([gram_v, eye, zero], axis=1)
    of_w = []
    for panel in range(panels):
        here = slice(panel * width, (panel + 1) * width)
        of_x = of_y[here]
        if panel:
            done = jnp.concatenate(of_w, axis=0)
            before = slice(0, panel * width)
            left = jnp.concatenate([done[:, here], gram_v[before, here]], axis=0)
            right = jnp.concatenate([of_v[before], done], axis=0)
            of_x = of_x - contract(left, right, 0, 0)
        factor = t_panels[panel]
        scaled = contract(factor, of_x, 0, 0)
        middle = contract(scaled[:, here], factor, 1, 0)
        of_w.append(scaled - 0.5 * contract(middle, of_v[here], 1, 0))
    return jnp.concatenate(of_w, axis=0)


def per_device(trailing, v_panels, t_panels):
    rows, cols = lax.axis_size("pr"), lax.axis_size("pc")
    ratio = rows // cols
    panels, width, share = v_panels.shape
    size = panels * width
    v_own = v_panels.reshape(size, share)
    moves = []
    for i in range(rows):
        for j in range(cols):
            moves.append((i * cols + j, ((i % ratio) * cols + j) * cols + i // ratio))

    def columns(own):
        return lax.all_gather(lax.ppermute(own, ("pr", "pc"), moves), "pr", axis=1, tiled=True)

    v_row = lax.all_gather(v_own, "pc", axis=1, tiled=True)
    v_col = columns(v_own)
    partial_y = contract(v_col, trailing, 1, 1, lax.Precision.HIGH)
    y_own = lax.psum_scatter(partial_y, "pc", scatter_dimension=1, tiled=True)
    y_row = lax.all_gather(y_own, "pc", axis=1, tiled=True)
    y_col = columns(y_own)
    grams = contract(v_own, jnp.concatenate([y_own, v_own], axis=0), 1, 1)
    grams = lax.psum(grams, ("pr", "pc"))
    coefs = small_coefficients(grams[:, :size], grams[:, size:], t_panels)
    of_v, of_y = coefs[:, size : 2 * size], coefs[:, 2 * size :]
    w_own = contract(of_v, v_own, 1, 0) + contract(of_y, y_own, 1, 0)
    left_v = contract(of_v + of_v.T, v_row, 1, 0) + contract(of_y, y_row, 1, 0)
    left_y = contract(of_y, v_row, 0, 0)
    left = jnp.concatenate([left_v, left_y], axis=0)
    right = jnp.concatenate([v_col, y_col], axis=0)
    matrix = trailing - contract(left, right, 0, 0, lax.Precision.HIGH)
    return (matrix, w_own.reshape(panels, width, share))


def solution(mesh):
    return jax.shard_map(
        per_device,
        mesh=mesh,
        in_specs=(P("pr", "pc"), P(None, None, ("pr", "pc")), P()),
        out_specs=(P("pr", "pc"), P(None, None, ("pr", "pc"))),
        check_vma=False,
    )
```

```python
import functools

import jax
import jax.numpy as jnp
from jax import lax
from jax.experimental import pallas as pl
from jax.experimental.pallas import tpu as pltpu
from jax.sharding import PartitionSpec as P

HIGHEST = lax.Precision.HIGHEST
MESH = pl.DeviceIdType.MESH
SIDE = 4


class Place:
    def __init__(self):
        pr, pc = lax.axis_index("pr"), lax.axis_index("pc")
        self.x, self.z = lax.rem(pr, SIDE), lax.div(pr, SIDE)
        self.y, self.core = lax.div(pc, 2), lax.rem(pc, 2)

    def at(self, x=0, y=0, z=0, other_core=False):
        far_x = lax.rem(self.x + x + SIDE, SIDE)
        far_y = lax.rem(self.y + y + SIDE, SIDE)
        far_z = lax.rem(self.z + z + SIDE, SIDE)
        core = 1 - self.core if other_core else self.core
        return far_z * SIDE + far_x, far_y * 2 + core

    def spread_to(self):
        block = lax.div(self.x, 2)
        keep = jnp.where(self.core == block, 1, 0)
        far_x = keep * self.x + (1 - keep) * (SIDE - 1 - self.x)
        return self.y * SIDE + far_x, self.z * 2 + block

    def spread_slot(self):
        block = lax.div(self.x, 2)
        return (self.x - 2 * block) * 8 + 2 * self.y + self.core

    def spread_from(self):
        keep = jnp.where(lax.div(self.x, 2) == self.core, 1, 0)
        far_x = keep * self.x + (1 - keep) * (SIDE - 1 - self.x)
        core = keep * self.core + (1 - keep) * (1 - self.core)
        return self.y * SIDE + far_x, self.z * 2 + core

    def column_slot(self, x=0, z=0):
        far_x = lax.rem(self.x + x + SIDE, SIDE)
        far_z = lax.rem(self.z + z + SIDE, SIDE)
        keep = jnp.where(lax.div(far_x, 2) == self.core, 1, 0)
        from_x = keep * far_x + (1 - keep) * (SIDE - 1 - far_x)
        core = keep * self.core + (1 - keep) * (1 - self.core)
        return (from_x - 2 * self.core) * 8 + 2 * far_z + core

    def row_slot(self, y=0, other_core=False):
        core = 1 - self.core if other_core else self.core
        return lax.rem(self.y + y + SIDE, SIDE) * 2 + core


class Mail:
    def __init__(self, send_sem, recv_sem):
        self.send_sem, self.recv_sem = send_sem, recv_sem
        self.count, self.sent = 0, []

    def number(self):
        self.count += 1
        return self.count - 1

    def copy(self, number, source, target, device):
        return pltpu.make_async_remote_copy(
            src_ref=source,
            dst_ref=target,
            send_sem=self.send_sem.at[number],
            recv_sem=self.recv_sem.at[number],
            device_id=device,
            device_id_type=MESH,
        )

    def send(self, number, source, target, device):
        copy = self.copy(number, source, target, device)
        copy.start()
        self.sent.append(copy)

    def receive(self, number, landed, device):
        self.copy(number, landed, landed, device).wait_recv()

    def finish(self):
        for copy in self.sent:
            copy.wait_send()


def is_here(device, place):
    pr, pc = place.at()
    return jnp.logical_and(device[0] == pr, device[1] == pc)


def spans(rows):
    half = rows // 2
    cut = -(-half // 16) * 8
    first, second = pl.ds(0, half), pl.ds(half, half)
    return (
        first,
        second,
        (pl.ds(0, cut), pl.ds(cut, half - cut)),
        (pl.ds(half, cut), pl.ds(half + cut, half - cut)),
    )


def gather(place, mail, own, row, col, local_sem):
    rows = own.shape[0]
    first, second, first_cut, second_cut = spans(rows)
    whole = pl.ds(0, rows)
    target = place.spread_to()
    stays = is_here(target, place)
    spread = mail.number()
    mine = place.column_slot()

    @pl.when(jnp.logical_not(stays))
    def _():
        mail.copy(spread, own, col.at[place.spread_slot()], target).start()

    @pl.when(stays)
    def _():
        pltpu.make_async_copy(own, col.at[mine], local_sem.at[0]).start()

    keep = pltpu.make_async_copy(own, row.at[place.row_slot()], local_sem.at[1])
    keep.start()

    up, down, up_on, down_on = (mail.number() for _ in range(4))
    cross = [mail.number() for _ in range(4)]
    partner = place.at(other_core=True)
    near_up, near_down = place.at(y=1), place.at(y=-1)
    here = place.row_slot()
    mail.send(up, own, row.at[here], near_up)
    mail.send(down, own, row.at[here], near_down)
    mail.send(cross[0], own, row.at[here], partner)

    def row_near():
        below, above = place.row_slot(y=-1), place.row_slot(y=1)
        mail.receive(up, row.at[below], near_down)
        mail.send(up_on, row.at[below, first], row.at[below, first], near_up)
        mail.send(cross[1], row.at[below], row.at[below], partner)
        mail.receive(down, row.at[above], near_up)
        mail.send(down_on, row.at[above, second], row.at[above, second], near_down)
        mail.send(cross[2], row.at[above], row.at[above], partner)

    def row_far():
        far = place.row_slot(y=2)
        mail.receive(up_on, row.at[far, first], near_down)
        mail.receive(down_on, row.at[far, second], near_up)
        mail.send(cross[3], row.at[far], row.at[far], partner)

    def row_end():
        for number, y in ((0, 0), (1, -1), (2, 1), (3, 2)):
            mail.receive(cross[number], row.at[place.row_slot(y=y, other_core=True)], partner)
        keep.wait()

    numbers = {}

    def number(*key):
        if key not in numbers:
            numbers[key] = mail.number()
        return numbers[key]

    def to(axis, step):
        return place.at(**{axis: step})

    def slot(axis, along, across):
        return place.column_slot(x=along, z=across) if axis == "x" else place.column_slot(x=across, z=along)

    def push(axis, step, half, across, span, along=0):
        ref = col.at[slot(axis, along, across), span]
        mail.send(number(axis, step, half, across, along), ref, ref, to(axis, step))

    def pull(axis, step, half, across, span, along=0):
        ref = col.at[slot(axis, along - step, across), span]
        mail.receive(number(axis, step, half, across, along), ref, to(axis, -step))

    halves = {"x": (first, first_cut), "z": (second, second_cut)}
    other = {"x": "z", "z": "x"}

    def start_column():
        @pl.when(jnp.logical_not(stays))
        def _():
            mail.copy(spread, own, col.at[mine], place.spread_from()).wait_recv()

        @pl.when(stays)
        def _():
            pltpu.make_async_copy(own, col.at[mine], local_sem.at[0]).wait()

        for axis in ("x", "z"):
            for step in (1, -1):
                push(axis, step, axis, 0, halves[axis][0])
        for axis in ("x", "z"):
            for step in (1, -1):
                push(axis, step, other[axis], 0, halves[other[axis]][0])

    def first_ring():
        for step, part in ((1, 0), (-1, 1)):
            for axis in ("x", "z"):
                span, cut = halves[axis]
                pull(axis, step, axis, 0, span)
                push(axis, step, axis, 0, cut[part], along=-step)
                for way in (1, -1):
                    push(other[axis], way, axis, -step, span)

    def second_ring_own():
        for step, part in ((1, 0), (-1, 1)):
            for axis in ("x", "z"):
                half = other[axis]
                span, cut = halves[half]
                pull(axis, step, half, 0, span)
                push(axis, step, half, 0, cut[part], along=-step)

    def first_ring_far():
        for axis in ("x", "z"):
            span, cut = halves[axis]
            for step, part in ((1, 0), (-1, 1)):
                pull(axis, step, axis, 0, cut[part], along=-step)
            for way in (1, -1):
                push(other[axis], way, axis, 2, span)

    def second_ring(across):
        for step, part in ((1, 0), (-1, 1)):
            for axis in ("x", "z"):
                half = other[axis]
                span, cut = halves[half]
                pull(axis, step, half, across, span)
                push(axis, step, half, across, cut[part], along=-step)

    def last():
        for across in (0, -1, 1, 2):
            for step, part in ((1, 0), (-1, 1)):
                for axis in ("x", "z"):
                    half = other[axis]
                    pull(axis, step, half, across, halves[half][1][part], along=-step)

    def finish():
        @pl.when(jnp.logical_not(stays))
        def _():
            mail.copy(spread, own, col.at[mine], target).wait_send()

    return {
        "row_near": row_near,
        "start_column": start_column,
        "first_ring": first_ring,
        "second_ring_own": second_ring_own,
        "row_far": row_far,
        "first_ring_far": first_ring_far,
        "second_ring_behind": functools.partial(second_ring, -1),
        "second_ring_ahead": functools.partial(second_ring, 1),
        "second_ring_far": functools.partial(second_ring, 2),
        "row_end": row_end,
        "last": last,
        "finish": finish,
    }


def enter(place, far):
    barrier = pltpu.get_barrier_semaphore()
    near = [place.at(x=1), place.at(x=-1), place.at(z=1), place.at(z=-1), place.at(y=1), place.at(y=-1)]
    near.append(place.at(other_core=True))
    if far:
        near += [place.at(x=2), place.at(y=2), place.at(z=2)]
    target, source = place.spread_to(), place.spread_from()
    moves = jnp.logical_not(is_here(target, place))
    for device in near:
        pl.semaphore_signal(barrier, inc=1, device_id=device, device_id_type=MESH)

    @pl.when(moves)
    def _():
        for device in (target, source):
            pl.semaphore_signal(barrier, inc=1, device_id=device, device_id_type=MESH)

    pl.semaphore_wait(barrier, len(near) + jnp.where(moves, 2, 0))


ORDER = (
    "start_column",
    "row_near",
    "first_ring",
    "second_ring_own",
    "row_far",
    "first_ring_far",
    "second_ring_behind",
    "second_ring_ahead",
    "second_ring_far",
    "row_end",
    "last",
    "finish",
)


def gather_kernel(own, row, col, send_sem, recv_sem, local_sem):
    place = Place()
    enter(place, False)
    mail = Mail(send_sem, recv_sem)
    steps = gather(place, mail, own, row, col, local_sem)
    for name in ORDER:
        steps[name]()
    mail.finish()


def hand_round(own):
    rows, lanes = own.shape
    return pl.pallas_call(
        gather_kernel,
        out_shape=(
            jax.ShapeDtypeStruct((8, rows, lanes), own.dtype),
            jax.ShapeDtypeStruct((16, rows, lanes), own.dtype),
        ),
        in_specs=[pl.BlockSpec(memory_space=pltpu.VMEM)],
        out_specs=[pl.BlockSpec(memory_space=pltpu.VMEM)] * 2,
        scratch_shapes=[
            pltpu.SemaphoreType.DMA((64,)),
            pltpu.SemaphoreType.DMA((64,)),
            pltpu.SemaphoreType.DMA((2,)),
        ],
        compiler_params=pltpu.CompilerParams(collective_id=0, has_side_effects=True),
        name="hand_round",
    )(own)


def total_kernel(partial_ref, grams_ref, row, col, total_ref, swap, sums, near, grams_swap, grams_sum, grams_y, grams_x, grams_z, send_sem, recv_sem, local_sem, own):
    place = Place()
    enter(place, True)
    mail = Mail(send_sem, recv_sem)
    rows = own.shape[0]
    first, second = pl.ds(0, rows // 2), pl.ds(rows // 2, rows // 2)
    partner = place.at(other_core=True)
    near_up, near_down = place.at(y=1), place.at(y=-1)

    half = grams_ref.shape[0] // 2
    part = half // SIDE
    cores = mail.number()
    mail.send(cores, grams_ref.at[pl.ds((1 - place.core) * half, half)], grams_swap, partner)
    across = {y: mail.number() for y in (2, 1, -1, 0)}
    for y, number in across.items():
        mail.send(number, partial_ref.at[place.row_slot(y=y, other_core=True)], swap.at[y % SIDE], partner)

    mail.receive(cores, grams_swap, partner)
    mine = pl.ds(pl.multiple_of(place.core * half, 8), half)
    grams_sum[pl.ds(0, half), :] = grams_ref[mine, :] + grams_swap[...]

    def exchange(axis, source, landing):
        numbers = [mail.number() for _ in range(1, SIDE)]
        for step in range(1, SIDE):
            mail.send(numbers[step - 1], source(step), landing.at[step - 1], place.at(**{axis: step}))

        def arrived():
            for step in range(1, SIDE):
                mail.receive(numbers[step - 1], landing.at[step - 1], place.at(**{axis: -step}))
            return landing[0] + landing[1] + landing[2]

        return arrived

    def quarter(step):
        return pl.ds(pl.multiple_of(lax.rem(place.y + step, SIDE) * part, 8), part)

    over_y = exchange("y", lambda step: grams_sum.at[quarter(step)], grams_y)

    def add_across(y):
        slot = y % SIDE
        mail.receive(across[y], swap.at[slot], partner)
        sums[slot, :, :] = partial_ref[place.row_slot(y=y)] + swap[slot]

    far_up, far_down, up_now, up_later, down_now, down_later = (mail.number() for _ in range(6))
    add_across(2)
    mail.send(far_up, sums.at[2, first], near.at[0, first], near_up)
    mail.send(far_down, sums.at[2, second], near.at[0, second], near_down)
    add_across(1)
    mail.send(up_now, sums.at[1, second], near.at[1, second], near_up)
    add_across(-1)
    mail.send(down_now, sums.at[3, first], near.at[2, first], near_down)
    add_across(0)
    grams_sum[pl.ds(half, part), :] = grams_sum[quarter(0), :] + over_y()
    over_x = exchange("x", lambda step: grams_sum.at[pl.ds(half, part)], grams_x)
    mail.receive(far_up, near.at[0, first], near_down)
    sums[1, first, :] = sums[1, first, :] + near[0, first, :]
    mail.send(up_later, sums.at[1, first], near.at[1, first], near_up)
    mail.receive(far_down, near.at[0, second], near_up)
    sums[3, second, :] = sums[3, second, :] + near[0, second, :]
    mail.send(down_later, sums.at[3, second], near.at[2, second], near_down)
    grams_sum[pl.ds(half + part, part), :] = grams_sum[pl.ds(half, part), :] + over_x()
    over_z = exchange("z", lambda step: grams_sum.at[pl.ds(half + part, part)], grams_z)
    mail.receive(up_now, near.at[1, second], near_down)
    mail.receive(down_now, near.at[2, first], near_up)
    mail.receive(up_later, near.at[1, first], near_down)
    mail.receive(down_later, near.at[2, second], near_up)
    own[...] = sums[0] + near[1] + near[2]

    steps = gather(place, mail, own, row, col, local_sem)

    def total_rows(y, other_core=False):
        core = 1 - place.core if other_core else place.core
        start = core * half + lax.rem(place.y + y + SIDE, SIDE) * part
        return total_ref.at[pl.ds(pl.multiple_of(start, 8), part)]

    start = place.core * half + place.y * part
    total_ref[pl.ds(pl.multiple_of(start, 8), part), :] = grams_sum[pl.ds(half + part, part), :] + over_z()
    back_y = [mail.number() for _ in range(1, SIDE)]
    back_core = [mail.number() for _ in range(SIDE)]
    for step in range(1, SIDE):
        mail.send(back_y[step - 1], total_rows(0), total_rows(0), place.at(y=step))
    mail.send(back_core[0], total_rows(0), total_rows(0), partner)

    def totals_on():
        for step in range(1, SIDE):
            mail.receive(back_y[step - 1], total_rows(-step), place.at(y=-step))
            mail.send(back_core[step], total_rows(-step), total_rows(-step), partner)

    def totals_end():
        for step in range(SIDE):
            mail.receive(back_core[step], total_rows(-step, True), partner)

    for name in ORDER:
        if name == "row_near":
            totals_on()
        if name == "row_far":
            totals_end()
        steps[name]()
    mail.finish()


def total_and_hand_round(partial, grams):
    _, rows, lanes = partial.shape
    parts = grams.shape[0] // 8
    f32 = jnp.float32
    return pl.pallas_call(
        total_kernel,
        out_shape=(
            jax.ShapeDtypeStruct((8, rows, lanes), f32),
            jax.ShapeDtypeStruct((16, rows, lanes), f32),
            jax.ShapeDtypeStruct(grams.shape, f32),
        ),
        in_specs=[pl.BlockSpec(memory_space=pltpu.VMEM)] * 2,
        out_specs=[pl.BlockSpec(memory_space=pltpu.VMEM)] * 3,
        scratch_shapes=[
            pltpu.VMEM((SIDE, rows, lanes), f32),
            pltpu.VMEM((SIDE, rows, lanes), f32),
            pltpu.VMEM((3, rows, lanes), f32),
            pltpu.VMEM((SIDE * parts, lanes), f32),
            pltpu.VMEM((6 * parts, lanes), f32),
            pltpu.VMEM((3, parts, lanes), f32),
            pltpu.VMEM((3, parts, lanes), f32),
            pltpu.VMEM((3, parts, lanes), f32),
            pltpu.SemaphoreType.DMA((96,)),
            pltpu.SemaphoreType.DMA((96,)),
            pltpu.SemaphoreType.DMA((2,)),
            pltpu.VMEM((rows, lanes), f32),
        ],
        compiler_params=pltpu.CompilerParams(collective_id=1, has_side_effects=True),
        name="total_and_hand_round",
    )(partial, grams)


def contract(left_side, right_side, left_dim, right_dim, precision=HIGHEST):
    return lax.dot_general(
        left_side,
        right_side,
        (((left_dim,), (right_dim,)), ((), ())),
        precision=precision,
        preferred_element_type=jnp.float32,
    )


WIDE = 256


def coefficients_kernel(panels, width, of_y_ref, of_v_ref, factor_ref, of_w_ref):
    for panel in range(panels):
        start = panel * width
        here = pl.ds(start, width)
        of_x = of_y_ref[here, :]
        if panel:
            before = pl.ds(0, start)
            of_x = of_x - contract(of_w_ref[before, here], of_v_ref[before, :], 0, 0)
            of_x = of_x - contract(of_v_ref[before, here], of_w_ref[before, :], 0, 0)
        factor = factor_ref[panel]
        scaled = contract(factor, of_x, 0, 0)
        middle = contract(scaled[:, start : start + width], factor, 1, 0)
        of_w_ref[here, :] = scaled - 0.5 * contract(middle, of_v_ref[here, :], 1, 0)


def coefficients(gram_y, gram_v, t_panels):
    panels, width, _ = t_panels.shape
    size = panels * width
    eye = jnp.eye(size, WIDE, dtype=jnp.float32)
    zero = jnp.zeros((size, WIDE), jnp.float32)

    def wide(block):
        return jnp.pad(block, ((0, 0), (0, WIDE - size)))

    of_w = pl.pallas_call(
        functools.partial(coefficients_kernel, panels, width),
        out_shape=jax.ShapeDtypeStruct((size, 3 * WIDE), jnp.float32),
        in_specs=[pl.BlockSpec(memory_space=pltpu.VMEM)] * 3,
        out_specs=pl.BlockSpec(memory_space=pltpu.VMEM),
        name="coefficients",
    )(
        jnp.concatenate([wide(gram_y), zero, eye], axis=1),
        jnp.concatenate([wide(gram_v), eye, zero], axis=1),
        t_panels,
    )
    return of_w[:, WIDE : WIDE + size], of_w[:, 2 * WIDE : 2 * WIDE + size]


def pack(share):
    rows = share.shape[-2] // 2
    tail = share[..., 128:]
    tail = jnp.concatenate([tail[..., :rows, :], tail[..., rows:, :]], axis=-1)
    return jnp.concatenate([share[..., :128], tail], axis=-2)


def unpack(packed):
    rows = packed.shape[-2] // 3
    tail = packed[..., 2 * rows :, :]
    tail = jnp.concatenate([tail[..., :64], tail[..., 64:]], axis=-2)
    return jnp.concatenate([packed[..., : 2 * rows, :], tail], axis=-1)


def per_device(trailing, v_panels, t_panels):
    panels, width, share = v_panels.shape
    size = panels * width
    v_own = v_panels.reshape(size, share).T
    v_row, v_col = hand_round(pack(v_own))
    v_row = unpack(v_row).reshape(-1, size)
    v_col = unpack(v_col).reshape(-1, size)
    partial = contract(trailing, v_col, 1, 0, lax.Precision.HIGH)
    grams = jnp.concatenate([contract(v_row, partial, 0, 0), contract(v_own, v_own, 0, 0)], axis=1)
    grams = jnp.concatenate([grams[:, :128], grams[:, 128:256], grams[:, 256:], jnp.zeros((64, 128), jnp.float32)])
    partial = pack(partial.reshape(-1, share, size))
    y_row, y_col, grams = total_and_hand_round(partial, grams)
    grams = jnp.concatenate([grams[:size], grams[size : 2 * size], grams[2 * size : 3 * size]], axis=1)
    of_v, of_y = coefficients(grams[:, :size], grams[:, size:], t_panels)
    me = lax.axis_index("pc")
    y_own = unpack(lax.dynamic_index_in_dim(y_row, me, 0, keepdims=False))
    y_row = unpack(y_row).reshape(-1, size)
    y_col = unpack(y_col).reshape(-1, size)
    w_own = contract(of_v, v_own, 1, 1) + contract(of_y, y_own, 1, 1)
    left_v = contract(v_row, of_v + of_v.T, 1, 0) + contract(y_row, of_y, 1, 1)
    left_y = contract(v_row, of_y, 1, 0)
    left = jnp.concatenate([left_v, left_y], axis=1)
    right = jnp.concatenate([v_col, y_col], axis=1)
    matrix = trailing - contract(left, right, 1, 1, lax.Precision.HIGH)
    return (matrix, w_own.reshape(panels, width, share))


def solution(mesh):
    return jax.shard_map(
        per_device,
        mesh=mesh,
        in_specs=(P("pr", "pc"), P(None, None, ("pr", "pc")), P()),
        out_specs=(P("pr", "pc"), P(None, None, ("pr", "pc"))),
        check_vma=False,
    )
```

```python
import functools

import jax
import jax.numpy as jnp
from jax import lax
from jax.experimental import pallas as pl
from jax.experimental.pallas import tpu as pltpu
from jax.sharding import PartitionSpec as P

HIGHEST = lax.Precision.HIGHEST
MESH = pl.DeviceIdType.MESH
SIDE = 4


class Place:
    def __init__(self):
        pr, pc = lax.axis_index("pr"), lax.axis_index("pc")
        self.x, self.z = lax.rem(pr, SIDE), lax.div(pr, SIDE)
        self.y, self.core = lax.div(pc, 2), lax.rem(pc, 2)

    def at(self, x=0, y=0, z=0, other_core=False):
        far_x = lax.rem(self.x + x + SIDE, SIDE)
        far_y = lax.rem(self.y + y + SIDE, SIDE)
        far_z = lax.rem(self.z + z + SIDE, SIDE)
        core = 1 - self.core if other_core else self.core
        return far_z * SIDE + far_x, far_y * 2 + core

    def spread_to(self):
        block = lax.div(self.x, 2)
        keep = jnp.where(self.core == block, 1, 0)
        far_x = keep * self.x + (1 - keep) * (SIDE - 1 - self.x)
        return self.y * SIDE + far_x, self.z * 2 + block

    def spread_slot(self):
        block = lax.div(self.x, 2)
        return (self.x - 2 * block) * 8 + 2 * self.y + self.core

    def spread_from(self):
        keep = jnp.where(lax.div(self.x, 2) == self.core, 1, 0)
        far_x = keep * self.x + (1 - keep) * (SIDE - 1 - self.x)
        core = keep * self.core + (1 - keep) * (1 - self.core)
        return self.y * SIDE + far_x, self.z * 2 + core

    def column_slot(self, x=0, z=0):
        far_x = lax.rem(self.x + x + SIDE, SIDE)
        far_z = lax.rem(self.z + z + SIDE, SIDE)
        keep = jnp.where(lax.div(far_x, 2) == self.core, 1, 0)
        from_x = keep * far_x + (1 - keep) * (SIDE - 1 - far_x)
        core = keep * self.core + (1 - keep) * (1 - self.core)
        return (from_x - 2 * self.core) * 8 + 2 * far_z + core

    def row_slot(self, y=0, other_core=False):
        core = 1 - self.core if other_core else self.core
        return lax.rem(self.y + y + SIDE, SIDE) * 2 + core


class Mail:
    def __init__(self, send_sem, recv_sem):
        self.send_sem, self.recv_sem = send_sem, recv_sem
        self.count, self.sent = 0, []

    def number(self):
        self.count += 1
        return self.count - 1

    def copy(self, number, source, target, device):
        return pltpu.make_async_remote_copy(
            src_ref=source,
            dst_ref=target,
            send_sem=self.send_sem.at[number],
            recv_sem=self.recv_sem.at[number],
            device_id=device,
            device_id_type=MESH,
        )

    def send(self, number, source, target, device):
        copy = self.copy(number, source, target, device)
        copy.start()
        self.sent.append(copy)

    def receive(self, number, landed, device):
        self.copy(number, landed, landed, device).wait_recv()

    def finish(self):
        for copy in self.sent:
            copy.wait_send()


def is_here(device, place):
    pr, pc = place.at()
    return jnp.logical_and(device[0] == pr, device[1] == pc)


def spans(rows):
    half = rows // 2
    cut = -(-half // 16) * 8
    first, second = pl.ds(0, half), pl.ds(half, half)
    return (
        first,
        second,
        (pl.ds(0, cut), pl.ds(cut, half - cut)),
        (pl.ds(half, cut), pl.ds(half + cut, half - cut)),
    )


def gather(place, mail, own, row, col, local_sem):
    rows = own.shape[0]
    first, second, first_cut, second_cut = spans(rows)
    whole = pl.ds(0, rows)
    target = place.spread_to()
    stays = is_here(target, place)
    spread = mail.number()
    mine = place.column_slot()

    @pl.when(jnp.logical_not(stays))
    def _():
        mail.copy(spread, own, col.at[place.spread_slot()], target).start()

    @pl.when(stays)
    def _():
        pltpu.make_async_copy(own, col.at[mine], local_sem.at[0]).start()

    keep = pltpu.make_async_copy(own, row.at[place.row_slot()], local_sem.at[1])
    keep.start()

    up, down, up_on, down_on = (mail.number() for _ in range(4))
    cross = [mail.number() for _ in range(4)]
    partner = place.at(other_core=True)
    near_up, near_down = place.at(y=1), place.at(y=-1)
    here = place.row_slot()
    mail.send(up, own, row.at[here], near_up)
    mail.send(down, own, row.at[here], near_down)
    mail.send(cross[0], own, row.at[here], partner)

    def row_near():
        below, above = place.row_slot(y=-1), place.row_slot(y=1)
        mail.receive(up, row.at[below], near_down)
        mail.send(up_on, row.at[below, first], row.at[below, first], near_up)
        mail.send(cross[1], row.at[below], row.at[below], partner)
        mail.receive(down, row.at[above], near_up)
        mail.send(down_on, row.at[above, second], row.at[above, second], near_down)
        mail.send(cross[2], row.at[above], row.at[above], partner)

    def row_far():
        far = place.row_slot(y=2)
        mail.receive(up_on, row.at[far, first], near_down)
        mail.receive(down_on, row.at[far, second], near_up)
        mail.send(cross[3], row.at[far], row.at[far], partner)

    def row_end():
        for number, y in ((0, 0), (1, -1), (2, 1), (3, 2)):
            mail.receive(cross[number], row.at[place.row_slot(y=y, other_core=True)], partner)
        keep.wait()

    numbers = {}

    def number(*key):
        if key not in numbers:
            numbers[key] = mail.number()
        return numbers[key]

    def to(axis, step):
        return place.at(**{axis: step})

    def slot(axis, along, across):
        return place.column_slot(x=along, z=across) if axis == "x" else place.column_slot(x=across, z=along)

    def push(axis, step, half, across, span, along=0):
        ref = col.at[slot(axis, along, across), span]
        mail.send(number(axis, step, half, across, along), ref, ref, to(axis, step))

    def pull(axis, step, half, across, span, along=0):
        ref = col.at[slot(axis, along - step, across), span]
        mail.receive(number(axis, step, half, across, along), ref, to(axis, -step))

    halves = {"x": (first, first_cut), "z": (second, second_cut)}
    other = {"x": "z", "z": "x"}

    def start_column():
        @pl.when(jnp.logical_not(stays))
        def _():
            mail.copy(spread, own, col.at[mine], place.spread_from()).wait_recv()

        @pl.when(stays)
        def _():
            pltpu.make_async_copy(own, col.at[mine], local_sem.at[0]).wait()

        for axis in ("x", "z"):
            for step in (1, -1):
                push(axis, step, axis, 0, halves[axis][0])
        for axis in ("x", "z"):
            for step in (1, -1):
                push(axis, step, other[axis], 0, halves[other[axis]][0])

    def first_ring():
        for step, part in ((1, 0), (-1, 1)):
            for axis in ("x", "z"):
                span, cut = halves[axis]
                pull(axis, step, axis, 0, span)
                push(axis, step, axis, 0, cut[part], along=-step)
                for way in (1, -1):
                    push(other[axis], way, axis, -step, span)

    def second_ring_own():
        for step, part in ((1, 0), (-1, 1)):
            for axis in ("x", "z"):
                half = other[axis]
                span, cut = halves[half]
                pull(axis, step, half, 0, span)
                push(axis, step, half, 0, cut[part], along=-step)

    def first_ring_far():
        for axis in ("x", "z"):
            span, cut = halves[axis]
            for step, part in ((1, 0), (-1, 1)):
                pull(axis, step, axis, 0, cut[part], along=-step)
            for way in (1, -1):
                push(other[axis], way, axis, 2, span)

    def second_ring(across):
        for step, part in ((1, 0), (-1, 1)):
            for axis in ("x", "z"):
                half = other[axis]
                span, cut = halves[half]
                pull(axis, step, half, across, span)
                push(axis, step, half, across, cut[part], along=-step)

    def last():
        for across in (0, -1, 1, 2):
            for step, part in ((1, 0), (-1, 1)):
                for axis in ("x", "z"):
                    half = other[axis]
                    pull(axis, step, half, across, halves[half][1][part], along=-step)

    def finish():
        @pl.when(jnp.logical_not(stays))
        def _():
            mail.copy(spread, own, col.at[mine], target).wait_send()

    return {
        "row_near": row_near,
        "start_column": start_column,
        "first_ring": first_ring,
        "second_ring_own": second_ring_own,
        "row_far": row_far,
        "first_ring_far": first_ring_far,
        "second_ring_behind": functools.partial(second_ring, -1),
        "second_ring_ahead": functools.partial(second_ring, 1),
        "second_ring_far": functools.partial(second_ring, 2),
        "row_end": row_end,
        "last": last,
        "finish": finish,
    }


def enter(place, far):
    barrier = pltpu.get_barrier_semaphore()
    near = [place.at(x=1), place.at(x=-1), place.at(z=1), place.at(z=-1), place.at(y=1), place.at(y=-1)]
    near.append(place.at(other_core=True))
    if far:
        near += [place.at(x=2), place.at(y=2), place.at(z=2)]
    target, source = place.spread_to(), place.spread_from()
    moves = jnp.logical_not(is_here(target, place))
    for device in near:
        pl.semaphore_signal(barrier, inc=1, device_id=device, device_id_type=MESH)

    @pl.when(moves)
    def _():
        for device in (target, source):
            pl.semaphore_signal(barrier, inc=1, device_id=device, device_id_type=MESH)

    pl.semaphore_wait(barrier, len(near) + jnp.where(moves, 2, 0))


ORDER = (
    "start_column",
    "row_near",
    "first_ring",
    "second_ring_own",
    "row_far",
    "first_ring_far",
    "second_ring_behind",
    "second_ring_ahead",
    "second_ring_far",
    "row_end",
    "last",
    "finish",
)


HIGH = lax.Precision.HIGH
BF16 = jnp.bfloat16
F32 = jnp.float32
LANES = 128
WIDE = 2 * LANES


def contract(left_side, right_side, left_dim, right_dim, precision=HIGHEST):
    return lax.dot_general(
        left_side,
        right_side,
        (((left_dim,), (right_dim,)), ((), ())),
        precision=precision,
        preferred_element_type=F32,
    )


def split(value):
    high = value.astype(BF16).astype(F32)
    return high, value - high


def left_lanes(shape):
    return lax.broadcasted_iota(jnp.int32, shape, len(shape) - 1) < LANES // 2


def swap_halves(value):
    return pltpu.roll(value, LANES // 2, 1)


def unpack(packed, wide, start):
    rows = packed.shape[0] // 3
    tail = packed[pl.ds(2 * rows, rows), :]
    left = left_lanes(tail.shape)
    wide[pl.ds(start, 2 * rows), 0:LANES] = packed[pl.ds(0, 2 * rows), :]
    wide[pl.ds(start, rows), LANES:WIDE] = jnp.where(left, tail, 0.0)
    wide[pl.ds(start + rows, rows), LANES:WIDE] = jnp.where(left, swap_halves(tail), 0.0)


def unpack_split(packed, parts, start, lane=0):
    rows = packed.shape[0] // 3
    high, low = split(packed[pl.ds(0, 2 * rows), :])
    parts[pl.ds(start, 2 * rows), lane : lane + LANES] = low.astype(BF16)
    parts[pl.ds(start, 2 * rows), lane + LANES : lane + 2 * LANES] = high.astype(BF16)
    high, low = split(packed[pl.ds(2 * rows, rows), :])
    left = left_lanes(high.shape)
    ends = slice(lane + 2 * LANES, lane + 3 * LANES)
    parts[pl.ds(start, rows), ends] = jnp.where(left, high, swap_halves(low)).astype(BF16)
    parts[pl.ds(start + rows, rows), ends] = jnp.where(left, swap_halves(high), low).astype(BF16)


CHUNK = 128
BLOCK = 320


def product_kernel(
    own, matrix, row, right, partial, grams, col, stage, high, low, row_wide, row_flat, product, send_sem, recv_sem, local_sem, stage_sem
):
    place = Place()
    rows = own.shape[0]
    share = 2 * rows // 3
    chunks = matrix.shape[0] // CHUNK

    def load(chunk):
        return pltpu.make_async_copy(matrix.at[pl.ds(chunk * CHUNK, CHUNK)], stage.at[chunk % 3], stage_sem.at[chunk % 3])

    for chunk in range(3):
        load(chunk).start()
    enter(place, False)
    mail = Mail(send_sem, recv_sem)
    steps = gather(place, mail, own, row, col, local_sem)
    todo = list(range(chunks))

    def convert():
        chunk = todo.pop(0)
        load(chunk).wait()
        top, rest = split(stage[chunk % 3])
        high[pl.ds(chunk * CHUNK, CHUNK), :] = top.astype(BF16)
        low[pl.ds(chunk * CHUNK, CHUNK), :] = rest.astype(BF16)
        if chunk + 3 < chunks:
            load(chunk + 3).start()

    def row_grams():
        for slot in range(8):
            unpack(row.at[slot], row_wide, slot * share)
        row_flat[...] = row_wide[...].T
        gram = contract(row_flat[0:192, :], row_wide[...], 1, 0, HIGH) * 0.125
        grams[384:576, :] = gram[:, 0:LANES]
        grams[576:768, :] = gram[:, LANES:WIDE]

    convert()
    convert()
    convert()
    for name in ORDER:
        steps[name]()
        if name == "row_end":
            while todo:
                convert()
            row_grams()
        elif name != "start_column" and todo:
            convert()
    for slot in range(16):
        unpack_split(col.at[slot], right, slot * share)

    @pl.loop(0, matrix.shape[0] // BLOCK)
    def _(block):
        here = pl.ds(pl.multiple_of(block * BLOCK, BLOCK), BLOCK)
        top = jnp.dot(high[here, :], right[...], preferred_element_type=F32)
        rest = jnp.dot(low[here, :], right[:, LANES:], preferred_element_type=F32)
        main = top[:, 0:LANES] + top[:, LANES : 2 * LANES] + rest[:, 0:LANES]
        tail = top[:, 2 * LANES :] + rest[:, LANES:]
        tail = tail + swap_halves(tail)
        product[here, 0:LANES] = main
        product[here, LANES:WIDE] = jnp.where(left_lanes(tail.shape), tail, 0.0)
        left = left_lanes((share // 2, LANES))
        for piece in range(BLOCK // share):
            slot = block * (BLOCK // share) + piece
            start = piece * share
            partial[slot, 0:share, :] = main[start : start + share]
            near, far = tail[start : start + share // 2], tail[start + share // 2 : start + share]
            partial[slot, share:, :] = jnp.where(left, near, far)

    gram = contract(row_flat[0:192, :], product[...], 1, 0, HIGH)
    grams[0:192, :] = gram[:, 0:LANES]
    grams[192:384, :] = gram[:, LANES:WIDE]
    mail.finish()


def in_vmem(count):
    return [pl.BlockSpec(memory_space=pltpu.VMEM)] * count


def product_call(own, matrix):
    rows, lanes = own.shape
    height, length = matrix.shape
    return pl.pallas_call(
        product_kernel,
        out_shape=(
            jax.ShapeDtypeStruct((8, rows, lanes), F32),
            jax.ShapeDtypeStruct((length, 3 * LANES), BF16),
            jax.ShapeDtypeStruct((8, rows, lanes), F32),
            jax.ShapeDtypeStruct((768, lanes), F32),
        ),
        in_specs=in_vmem(1) + [pl.BlockSpec(memory_space=pl.ANY)],
        out_specs=in_vmem(4),
        scratch_shapes=[
            pltpu.VMEM((16, rows, lanes), F32),
            pltpu.VMEM((3, CHUNK, length), F32),
            pltpu.VMEM((height, length), BF16),
            pltpu.VMEM((height, length), BF16),
            pltpu.VMEM((height, WIDE), F32),
            pltpu.VMEM((WIDE, height), F32),
            pltpu.VMEM((height, WIDE), F32),
            pltpu.SemaphoreType.DMA((64,)),
            pltpu.SemaphoreType.DMA((64,)),
            pltpu.SemaphoreType.DMA((2,)),
            pltpu.SemaphoreType.DMA((3,)),
        ],
        compiler_params=pltpu.CompilerParams(collective_id=0, has_side_effects=True, vmem_limit_bytes=60 * 1024 * 1024),
        name="v_shares_and_product",
    )(own, matrix)


def coefficient_steps(panels, width, total_ref, factor_ref, of_y, of_v, of_w):
    size = panels * width

    def begin():
        rows = lax.broadcasted_iota(jnp.int32, (size, WIDE), 0)
        cols = lax.broadcasted_iota(jnp.int32, (size, WIDE), 1)
        eye = jnp.where(rows == cols, 1.0, 0.0)
        zero = jnp.zeros((size, WIDE), F32)
        for ref, first, at in ((of_y, 0, 2), (of_v, 2 * size, 1)):
            ref[:, 0:LANES] = total_ref[pl.ds(first, size), :]
            ref[:, LANES:WIDE] = total_ref[pl.ds(first + size, size), :]
            ref[:, WIDE * at : WIDE * (at + 1)] = eye
            ref[:, WIDE * (3 - at) : WIDE * (4 - at)] = zero

    def step(panel):
        start = panel * width
        here = slice(start, start + width)
        of_x = of_y[here, :]
        if panel:
            before = slice(0, start)
            of_x = of_x - contract(of_w[before, here], of_v[before, :], 0, 0)
            of_x = of_x - contract(of_v[before, here], of_w[before, :], 0, 0)
        factor = factor_ref[panel]
        scaled = contract(factor, of_x, 0, 0)
        middle = contract(scaled[:, here], factor, 1, 0)
        of_w[here, :] = scaled - 0.5 * contract(middle, of_v[here, :], 1, 0)

    return begin, step


def total_kernel(
    panels,
    width,
    partial_ref,
    grams_ref,
    row_v,
    right_v,
    factor_ref,
    right,
    left_high,
    left_low,
    w_ref,
    row,
    col,
    total_ref,
    swap,
    sums,
    near,
    grams_swap,
    grams_sum,
    grams_y,
    grams_x,
    grams_z,
    own,
    of_y,
    of_v,
    of_w,
    mixing,
    share_v,
    share_y,
    send_sem,
    recv_sem,
    local_sem,
):
    place = Place()
    enter(place, True)
    mail = Mail(send_sem, recv_sem)
    rows = own.shape[0]
    first, second = pl.ds(0, rows // 2), pl.ds(rows // 2, rows // 2)
    partner = place.at(other_core=True)
    near_up, near_down = place.at(y=1), place.at(y=-1)

    half = grams_ref.shape[0] // 2
    part = half // SIDE
    cores = mail.number()
    mail.send(cores, grams_ref.at[pl.ds((1 - place.core) * half, half)], grams_swap, partner)
    across = {y: mail.number() for y in (2, 1, -1, 0)}
    for y, number in across.items():
        mail.send(number, partial_ref.at[place.row_slot(y=y, other_core=True)], swap.at[y % SIDE], partner)

    mail.receive(cores, grams_swap, partner)
    mine = pl.ds(pl.multiple_of(place.core * half, 8), half)
    grams_sum[pl.ds(0, half), :] = grams_ref[mine, :] + grams_swap[...]

    def exchange(axis, source, landing):
        numbers = [mail.number() for _ in range(1, SIDE)]
        for step in range(1, SIDE):
            mail.send(numbers[step - 1], source(step), landing.at[step - 1], place.at(**{axis: step}))

        def arrived():
            for step in range(1, SIDE):
                mail.receive(numbers[step - 1], landing.at[step - 1], place.at(**{axis: -step}))
            return landing[0] + landing[1] + landing[2]

        return arrived

    def quarter(step):
        return pl.ds(pl.multiple_of(lax.rem(place.y + step, SIDE) * part, 8), part)

    over_y = exchange("y", lambda step: grams_sum.at[quarter(step)], grams_y)

    def add_across(y):
        slot = y % SIDE
        mail.receive(across[y], swap.at[slot], partner)
        sums[slot, :, :] = partial_ref[place.row_slot(y=y)] + swap[slot]

    far_up, far_down, up_now, up_later, down_now, down_later = (mail.number() for _ in range(6))
    add_across(2)
    mail.send(far_up, sums.at[2, first], near.at[0, first], near_up)
    mail.send(far_down, sums.at[2, second], near.at[0, second], near_down)
    add_across(1)
    mail.send(up_now, sums.at[1, second], near.at[1, second], near_up)
    add_across(-1)
    mail.send(down_now, sums.at[3, first], near.at[2, first], near_down)
    add_across(0)
    grams_sum[pl.ds(half, part), :] = grams_sum[quarter(0), :] + over_y()
    over_x = exchange("x", lambda step: grams_sum.at[pl.ds(half, part)], grams_x)
    mail.receive(far_up, near.at[0, first], near_down)
    sums[1, first, :] = sums[1, first, :] + near[0, first, :]
    mail.send(up_later, sums.at[1, first], near.at[1, first], near_up)
    mail.receive(far_down, near.at[0, second], near_up)
    sums[3, second, :] = sums[3, second, :] + near[0, second, :]
    mail.send(down_later, sums.at[3, second], near.at[2, second], near_down)
    grams_sum[pl.ds(half + part, part), :] = grams_sum[pl.ds(half, part), :] + over_x()
    over_z = exchange("z", lambda step: grams_sum.at[pl.ds(half + part, part)], grams_z)
    mail.receive(up_now, near.at[1, second], near_down)
    mail.receive(down_now, near.at[2, first], near_up)
    mail.receive(up_later, near.at[1, first], near_down)
    mail.receive(down_later, near.at[2, second], near_up)
    own[...] = sums[0] + near[1] + near[2]

    steps = gather(place, mail, own, row, col, local_sem)

    def total_rows(y, other_core=False):
        core = 1 - place.core if other_core else place.core
        start = core * half + lax.rem(place.y + y + SIDE, SIDE) * part
        return total_ref.at[pl.ds(pl.multiple_of(start, 8), part)]

    start = place.core * half + place.y * part
    total_ref[pl.ds(pl.multiple_of(start, 8), part), :] = grams_sum[pl.ds(half + part, part), :] + over_z()
    back_y = [mail.number() for _ in range(1, SIDE)]
    back_core = [mail.number() for _ in range(SIDE)]
    for step in range(1, SIDE):
        mail.send(back_y[step - 1], total_rows(0), total_rows(0), place.at(y=step))
    mail.send(back_core[0], total_rows(0), total_rows(0), partner)

    def totals_on():
        for step in range(1, SIDE):
            mail.receive(back_y[step - 1], total_rows(-step), place.at(y=-step))
            mail.send(back_core[step], total_rows(-step), total_rows(-step), partner)

    def totals_end():
        for step in range(SIDE):
            mail.receive(back_core[step], total_rows(-step, True), partner)

    begin, step = coefficient_steps(panels, width, total_ref, factor_ref, of_y, of_v, of_w)
    size = panels * width
    share = 2 * own.shape[0] // 3

    def mix():
        mixing[...] = jnp.zeros_like(mixing)
        of_d, of_c = of_w[:, WIDE : 2 * WIDE], of_w[:, 2 * WIDE :]
        mixing[0:size, 0:WIDE] = of_d
        mixing[:, 0:WIDE] = mixing[:, 0:WIDE] + mixing[:, 0:WIDE].T
        mixing[0:size, WIDE:] = of_c

    def store_left(value, start, lane, low_lane):
        left = left_lanes((share, LANES))
        for at in range(2):
            top, rest = split(value[:, at * LANES : (at + 1) * LANES])
            if at:
                top = jnp.where(left, top, swap_halves(top))
                rest = jnp.where(left, rest, swap_halves(rest))
            here = pl.ds(start, share)
            low_here = slice(low_lane + at * LANES, low_lane + (at + 1) * LANES)
            left_low[here, low_here] = rest.astype(BF16)
            if not at:
                left_high[here, lane : lane + LANES] = top.astype(BF16)
            left_high[here, lane + (at + 1) * LANES : lane + (at + 2) * LANES] = top.astype(BF16)

    def left_rows(slot):
        unpack(row_v.at[slot], share_v, 0)
        unpack(row.at[slot], share_y, 0)
        of_right_v = contract(share_v[...], mixing[:, 0:WIDE], 1, 0, HIGH)
        of_right_v = of_right_v + contract(share_y[...], mixing[:, WIDE:], 1, 1, HIGH)
        of_right_y = contract(share_v[...], mixing[:, WIDE:], 1, 0, HIGH)
        store_left(of_right_v, slot * share, 0, 0)
        store_left(of_right_y, slot * share, 3 * LANES, 2 * LANES)

    def w_rows():
        unpack(row_v.at[place.row_slot()], share_v, 0)
        unpack(own, share_y, 0)
        w_ref[...] = contract(of_w[:, WIDE : 2 * WIDE], share_v[...], 1, 1, HIGH)
        w_ref[...] = w_ref[...] + contract(of_w[:, 2 * WIDE :], share_y[...], 1, 1, HIGH)

    after = {
        "second_ring_own": [begin, lambda: step(0)],
        "row_far": [lambda: step(1), lambda: step(2)],
        "first_ring_far": [lambda: step(3)],
        "second_ring_behind": [lambda: step(4)],
        "second_ring_ahead": [lambda: step(5), mix],
        "second_ring_far": [w_rows],
        "row_end": [functools.partial(left_rows, slot) for slot in range(8)],
    }
    right[:, 0 : 3 * LANES] = right_v[...]
    for name in ORDER:
        if name == "row_near":
            totals_on()
        steps[name]()
        if name == "first_ring":
            totals_end()
        for work in after.get(name, ()):
            work()
    for slot in range(16):
        unpack_split(col.at[slot], right, slot * share, 3 * LANES)
    mail.finish()


def total_call(partial, grams, row_v, right_v, factors):
    _, rows, lanes = partial.shape
    panels, width, _ = factors.shape
    size = panels * width
    share = 2 * rows // 3
    length = right_v.shape[0]
    parts = grams.shape[0] // 8
    return pl.pallas_call(
        functools.partial(total_kernel, panels, width),
        out_shape=(
            jax.ShapeDtypeStruct((length, 6 * LANES), BF16),
            jax.ShapeDtypeStruct((8 * share, 6 * LANES), BF16),
            jax.ShapeDtypeStruct((8 * share, 4 * LANES), BF16),
            jax.ShapeDtypeStruct((size, share), F32),
        ),
        in_specs=in_vmem(5),
        out_specs=in_vmem(4),
        scratch_shapes=[
            pltpu.VMEM((8, rows, lanes), F32),
            pltpu.VMEM((16, rows, lanes), F32),
            pltpu.VMEM(grams.shape, F32),
            pltpu.VMEM((SIDE, rows, lanes), F32),
            pltpu.VMEM((SIDE, rows, lanes), F32),
            pltpu.VMEM((3, rows, lanes), F32),
            pltpu.VMEM((SIDE * parts, lanes), F32),
            pltpu.VMEM((6 * parts, lanes), F32),
            pltpu.VMEM((3, parts, lanes), F32),
            pltpu.VMEM((3, parts, lanes), F32),
            pltpu.VMEM((3, parts, lanes), F32),
            pltpu.VMEM((rows, lanes), F32),
            pltpu.VMEM((size, 3 * WIDE), F32),
            pltpu.VMEM((size, 3 * WIDE), F32),
            pltpu.VMEM((size, 3 * WIDE), F32),
            pltpu.VMEM((WIDE, 2 * WIDE), F32),
            pltpu.VMEM((share, WIDE), F32),
            pltpu.VMEM((share, WIDE), F32),
            pltpu.SemaphoreType.DMA((96,)),
            pltpu.SemaphoreType.DMA((96,)),
            pltpu.SemaphoreType.DMA((2,)),
        ],
        compiler_params=pltpu.CompilerParams(collective_id=1, has_side_effects=True, vmem_limit_bytes=60 * 1024 * 1024),
        name="totals_and_factors",
    )(partial, grams, row_v, right_v, factors)


TILE = 256


def update_kernel(matrix_ref, right_ref, high_ref, low_ref, w_in, out_ref, w_out):
    right = right_ref[...]
    change = contract(high_ref[...], right, 1, 1, None)
    low_v, low_y = low_ref[:, 0 : 2 * LANES], low_ref[:, 2 * LANES :]
    change = change + contract(low_v, right[:, LANES : 3 * LANES], 1, 1, None)
    change = change + contract(low_y, right[:, 4 * LANES :], 1, 1, None)
    out_ref[...] = matrix_ref[...] - change
    w_out[...] = w_in[...]


def update_call(matrix, right, left_high, left_low, w):
    height, length = matrix.shape

    def whole(array):
        return pl.BlockSpec(array.shape, lambda tile: (0, 0), pipeline_mode=pl.Buffered(1))

    return pl.pallas_call(
        update_kernel,
        grid=(length // TILE,),
        out_shape=(jax.ShapeDtypeStruct(matrix.shape, F32), jax.ShapeDtypeStruct(w.shape, F32)),
        in_specs=[
            pl.BlockSpec((height, TILE), lambda tile: (0, tile)),
            pl.BlockSpec((TILE, right.shape[1]), lambda tile: (tile, 0)),
            whole(left_high),
            whole(left_low),
            whole(w),
        ],
        out_specs=[pl.BlockSpec((height, TILE), lambda tile: (0, tile)), pl.BlockSpec(w.shape, lambda tile: (0, 0))],
        compiler_params=pltpu.CompilerParams(dimension_semantics=("arbitrary",), vmem_limit_bytes=60 * 1024 * 1024),
        name="update",
    )(matrix, right, left_high, left_low, w)


def pack(share):
    rows = share.shape[0] // 2
    tail = share[:, LANES:]
    tail = jnp.concatenate([tail[:rows], tail[rows:]], axis=1)
    return jnp.concatenate([share[:, :LANES], tail], axis=0)


def per_device(trailing, v_panels, t_panels):
    panels, width, share = v_panels.shape
    size = panels * width
    own = pack(v_panels.reshape(size, share).T)
    row_v, right_v, partial, grams = product_call(own, trailing)
    right, left_high, left_low, w = total_call(partial, grams, row_v, right_v, t_panels)
    matrix, w = update_call(trailing, right, left_high, left_low, w)
    return (matrix, w.reshape(panels, width, share))


def solution(mesh):
    return jax.shard_map(
        per_device,
        mesh=mesh,
        in_specs=(P("pr", "pc"), P(None, None, ("pr", "pc")), P()),
        out_specs=(P("pr", "pc"), P(None, None, ("pr", "pc"))),
        check_vma=False,
    )
```

```python
import functools

import jax
import jax.numpy as jnp
from jax import lax
from jax.experimental import pallas as pl
from jax.experimental.pallas import tpu as pltpu
from jax.sharding import PartitionSpec as P

HIGHEST = lax.Precision.HIGHEST
MESH = pl.DeviceIdType.MESH
SIDE = 4


class Place:
    def __init__(self):
        pr, pc = lax.axis_index("pr"), lax.axis_index("pc")
        self.x, self.z = lax.rem(pr, SIDE), lax.div(pr, SIDE)
        self.y, self.core = lax.div(pc, 2), lax.rem(pc, 2)

    def at(self, x=0, y=0, z=0, other_core=False):
        far_x = lax.rem(self.x + x + SIDE, SIDE)
        far_y = lax.rem(self.y + y + SIDE, SIDE)
        far_z = lax.rem(self.z + z + SIDE, SIDE)
        core = 1 - self.core if other_core else self.core
        return far_z * SIDE + far_x, far_y * 2 + core

    def spread_to(self):
        block = lax.div(self.x, 2)
        keep = jnp.where(self.core == block, 1, 0)
        far_x = keep * self.x + (1 - keep) * (SIDE - 1 - self.x)
        return lax.rem(self.y + self.z, SIDE) * SIDE + far_x, self.z * 2 + block

    def spread_slot(self):
        block = lax.div(self.x, 2)
        return (self.x - 2 * block) * 8 + 2 * self.y + self.core

    def spread_from(self):
        keep = jnp.where(lax.div(self.x, 2) == self.core, 1, 0)
        far_x = keep * self.x + (1 - keep) * (SIDE - 1 - self.x)
        core = keep * self.core + (1 - keep) * (1 - self.core)
        return self.y * SIDE + far_x, lax.rem(self.z - self.y + SIDE, SIDE) * 2 + core

    def column_slot(self, x=0, z=0):
        far_x = lax.rem(self.x + x + SIDE, SIDE)
        far_z = lax.rem(self.z + z + SIDE, SIDE)
        keep = jnp.where(lax.div(far_x, 2) == self.core, 1, 0)
        from_x = keep * far_x + (1 - keep) * (SIDE - 1 - far_x)
        core = keep * self.core + (1 - keep) * (1 - self.core)
        return (from_x - 2 * self.core) * 8 + 2 * lax.rem(far_z - self.y + SIDE, SIDE) + core

    def row_slot(self, y=0, other_core=False):
        core = 1 - self.core if other_core else self.core
        return lax.rem(self.y + y + SIDE, SIDE) * 2 + core


class Mail:
    def __init__(self, send_sem, recv_sem):
        self.send_sem, self.recv_sem = send_sem, recv_sem
        self.count, self.sent = 0, []

    def number(self):
        self.count += 1
        return self.count - 1

    def copy(self, number, source, target, device):
        return pltpu.make_async_remote_copy(
            src_ref=source,
            dst_ref=target,
            send_sem=self.send_sem.at[number],
            recv_sem=self.recv_sem.at[number],
            device_id=device,
            device_id_type=MESH,
        )

    def send(self, number, source, target, device):
        copy = self.copy(number, source, target, device)
        copy.start()
        self.sent.append(copy)

    def receive(self, number, landed, device):
        self.copy(number, landed, landed, device).wait_recv()

    def finish(self):
        for copy in self.sent:
            copy.wait_send()


def is_here(device, place):
    pr, pc = place.at()
    return jnp.logical_and(device[0] == pr, device[1] == pc)


def spans(rows):
    half = rows // 2
    cut = -(-half // 16) * 8
    first, second = pl.ds(0, half), pl.ds(half, half)
    return (
        first,
        second,
        (pl.ds(0, cut), pl.ds(cut, half - cut)),
        (pl.ds(half, cut), pl.ds(half + cut, half - cut)),
    )


class Spread:
    def __init__(self, place, mail, back=False):
        self.mail, self.number = mail, mail.number()
        self.target = place.spread_from() if back else place.spread_to()
        self.source = place.spread_to() if back else place.spread_from()
        self.stays = is_here(self.target, place)

    def start(self, own, landing, landed, local_sem):
        self.own, self.landed = own, landed
        self.local = pltpu.make_async_copy(own, landed, local_sem)
        self.remote = self.mail.copy(self.number, own, landing, self.target)

        @pl.when(jnp.logical_not(self.stays))
        def _():
            self.remote.start()

        @pl.when(self.stays)
        def _():
            self.local.start()

    def arrived(self):
        @pl.when(jnp.logical_not(self.stays))
        def _():
            self.mail.copy(self.number, self.own, self.landed, self.source).wait_recv()

        @pl.when(self.stays)
        def _():
            self.local.wait()

    def finish(self):
        @pl.when(jnp.logical_not(self.stays))
        def _():
            self.remote.wait_send()


class RowRing:
    def __init__(self, place, mail, own, row, local_sem):
        self.place, self.mail, self.own, self.row = place, mail, own, row
        self.first, self.second, _, _ = spans(own.shape[0])
        self.up, self.down, self.up_on, self.down_on = (mail.number() for _ in range(4))
        self.cross = [mail.number() for _ in range(4)]
        self.partner = place.at(other_core=True)
        self.near_up, self.near_down = place.at(y=1), place.at(y=-1)
        self.keep = pltpu.make_async_copy(own, row.at[place.row_slot()], local_sem)

    def start(self):
        here = self.row.at[self.place.row_slot()]
        self.keep.start()
        self.mail.send(self.up, self.own, here, self.near_up)
        self.mail.send(self.down, self.own, here, self.near_down)
        self.mail.send(self.cross[0], self.own, here, self.partner)

    def near(self):
        mail, row = self.mail, self.row
        below, above = self.place.row_slot(y=-1), self.place.row_slot(y=1)
        mail.receive(self.up, row.at[below], self.near_down)
        mail.send(self.up_on, row.at[below, self.first], row.at[below, self.first], self.near_up)
        mail.send(self.cross[1], row.at[below], row.at[below], self.partner)
        mail.receive(self.down, row.at[above], self.near_up)
        mail.send(self.down_on, row.at[above, self.second], row.at[above, self.second], self.near_down)
        mail.send(self.cross[2], row.at[above], row.at[above], self.partner)

    def far(self):
        mail, row = self.mail, self.row
        far = self.place.row_slot(y=2)
        mail.receive(self.up_on, row.at[far, self.first], self.near_down)
        mail.receive(self.down_on, row.at[far, self.second], self.near_up)
        mail.send(self.cross[3], row.at[far], row.at[far], self.partner)

    def end(self):
        for number, y in ((0, 0), (1, -1), (2, 1), (3, 2)):
            landed = self.row.at[self.place.row_slot(y=y, other_core=True)]
            self.mail.receive(self.cross[number], landed, self.partner)
        self.keep.wait()


OTHER = {"x": "z", "z": "x"}


class ColumnRings:
    def __init__(self, place, mail, col):
        self.place, self.mail, self.col, self.numbers = place, mail, col, {}
        first, second, first_cut, second_cut = spans(col.shape[1])
        self.halves = {"x": (first, first_cut), "z": (second, second_cut)}

    def number(self, *key):
        if key not in self.numbers:
            self.numbers[key] = self.mail.number()
        return self.numbers[key]

    def ref(self, axis, along, across, span):
        x, z = (along, across) if axis == "x" else (across, along)
        return self.col.at[self.place.column_slot(x=x, z=z), span]

    def to(self, axis, step):
        return self.place.at(**{axis: step})

    def push(self, axis, step, half, across, span, along=0):
        ref = self.ref(axis, along, across, span)
        self.mail.send(self.number(axis, step, half, across, along), ref, ref, self.to(axis, step))

    def pull(self, axis, step, half, across, span, along=0):
        ref = self.ref(axis, along - step, across, span)
        self.mail.receive(self.number(axis, step, half, across, along), ref, self.to(axis, -step))

    def pass_on(self, axis, half, across):
        span = self.halves[half][0]
        for step in (1, -1):
            self.push(axis, step, half, across, span)
        if half == axis:
            ref = self.ref(axis, 0, across, span)
            self.mail.send(self.number(axis, "far", half, across), ref, ref, self.to(axis, 2))

    def take(self, axis, step, half, across):
        self.pull(axis, step, half, across, self.halves[half][0])
        if half != axis:
            self.push(axis, step, half, across, self.halves[half][1][0 if step == 1 else 1], along=-step)

    def take_far(self, axis, half, across):
        if half == axis:
            ref = self.ref(axis, 2, across, self.halves[half][0])
            self.mail.receive(self.number(axis, "far", half, across), ref, self.to(axis, 2))
        else:
            for step, part in ((1, 0), (-1, 1)):
                self.pull(axis, step, half, across, self.halves[half][1][part], along=-step)

    def start(self):
        for axis in ("x", "z"):
            self.pass_on(axis, axis, 0)
        for axis in ("x", "z"):
            self.pass_on(axis, OTHER[axis], 0)

    def first_ring(self):
        for step in (1, -1):
            for axis in ("x", "z"):
                self.take(axis, step, axis, 0)
                self.pass_on(OTHER[axis], axis, -step)

    def first_ring_far(self):
        for axis in ("x", "z"):
            self.take_far(axis, axis, 0)
            self.pass_on(OTHER[axis], axis, 2)

    def second_ring(self, across):
        for step in (1, -1):
            for axis in ("x", "z"):
                self.take(axis, step, OTHER[axis], across)

    def last(self):
        for across in (0, -1, 1, 2):
            for axis in ("x", "z"):
                self.take_far(axis, OTHER[axis], across)


def enter(place, far):
    barrier = pltpu.get_barrier_semaphore()
    near = [place.at(x=1), place.at(x=-1), place.at(z=1), place.at(z=-1), place.at(y=1), place.at(y=-1)]
    near.append(place.at(other_core=True))
    if far:
        near += [place.at(x=2), place.at(y=2), place.at(z=2)]
    target, source = place.spread_to(), place.spread_from()
    moves = jnp.logical_not(is_here(target, place))
    for device in near:
        pl.semaphore_signal(barrier, inc=1, device_id=device, device_id_type=MESH)

    @pl.when(moves)
    def _():
        for device in (target, source):
            pl.semaphore_signal(barrier, inc=1, device_id=device, device_id_type=MESH)

    pl.semaphore_wait(barrier, len(near) + jnp.where(moves, 2, 0))


HIGH = lax.Precision.HIGH
BF16 = jnp.bfloat16
F32 = jnp.float32
LANES = 128
WIDE = 2 * LANES


def contract(left_side, right_side, left_dim, right_dim, precision=HIGHEST):
    return lax.dot_general(
        left_side,
        right_side,
        (((left_dim,), (right_dim,)), ((), ())),
        precision=precision,
        preferred_element_type=F32,
    )


def split(value):
    high = value.astype(BF16).astype(F32)
    return high, value - high


def left_lanes(shape):
    return lax.broadcasted_iota(jnp.int32, shape, len(shape) - 1) < LANES // 2


def swap_halves(value):
    return pltpu.roll(value, LANES // 2, 1)


def unpack(packed, wide, start):
    rows = packed.shape[0] // 3
    tail = packed[pl.ds(2 * rows, rows), :]
    left = left_lanes(tail.shape)
    wide[pl.ds(start, 2 * rows), 0:LANES] = packed[pl.ds(0, 2 * rows), :]
    wide[pl.ds(start, rows), LANES:WIDE] = jnp.where(left, tail, 0.0)
    wide[pl.ds(start + rows, rows), LANES:WIDE] = jnp.where(left, swap_halves(tail), 0.0)


def unpack_split(packed, parts, start, lane=0):
    rows = packed.shape[0] // 3
    high, low = split(packed[pl.ds(0, 2 * rows), :])
    parts[pl.ds(start, 2 * rows), lane : lane + LANES] = low.astype(BF16)
    parts[pl.ds(start, 2 * rows), lane + LANES : lane + 2 * LANES] = high.astype(BF16)
    high, low = split(packed[pl.ds(2 * rows, rows), :])
    left = left_lanes(high.shape)
    ends = slice(lane + 2 * LANES, lane + 3 * LANES)
    parts[pl.ds(start, rows), ends] = jnp.where(left, high, swap_halves(low)).astype(BF16)
    parts[pl.ds(start + rows, rows), ends] = jnp.where(left, swap_halves(high), low).astype(BF16)


def coefficient_steps(panels, width, total_ref, factor_ref, of_y, of_v, of_w):
    size = panels * width

    def begin():
        rows = lax.broadcasted_iota(jnp.int32, (size, WIDE), 0)
        cols = lax.broadcasted_iota(jnp.int32, (size, WIDE), 1)
        eye = jnp.where(rows == cols, 1.0, 0.0)
        zero = jnp.zeros((size, WIDE), F32)
        for ref, first, at in ((of_y, 0, 2), (of_v, 2 * size, 1)):
            ref[:, 0:LANES] = total_ref[pl.ds(first, size), :]
            ref[:, LANES:WIDE] = total_ref[pl.ds(first + size, size), :]
            ref[:, WIDE * at : WIDE * (at + 1)] = eye
            ref[:, WIDE * (3 - at) : WIDE * (4 - at)] = zero

    def step(panel):
        start = panel * width
        here = slice(start, start + width)
        of_x = of_y[here, :]
        if panel:
            before = slice(0, start)
            of_x = of_x - contract(of_w[before, here], of_v[before, :], 0, 0)
            of_x = of_x - contract(of_v[before, here], of_w[before, :], 0, 0)
        factor = factor_ref[panel]
        scaled = contract(factor, of_x, 0, 0)
        middle = contract(scaled[:, here], factor, 1, 0)
        of_w[here, :] = scaled - 0.5 * contract(middle, of_v[here, :], 1, 0)

    return begin, step


CHUNK = 128


def factors_kernel(
    panels,
    width,
    v_ref,
    matrix,
    factors,
    right,
    left_high,
    left_low,
    w_ref,
    stage,
    high,
    low,
    row_v,
    row_y,
    col_v,
    col_y,
    row_wide,
    flat_v,
    wide_y,
    partial,
    swap,
    sums,
    near,
    share_sum,
    own,
    factor_ref,
    grams_ref,
    total_ref,
    grams_swap,
    grams_sum,
    grams_y,
    grams_x,
    grams_z,
    of_y,
    of_v,
    of_w,
    mixing,
    share_v,
    share_y,
    send_sem,
    recv_sem,
    local_sem,
    stage_sem,
):
    place = Place()
    rows = own.shape[0]
    size = panels * width
    share = v_ref.shape[1]
    chunks = matrix.shape[0] // CHUNK
    partner = place.at(other_core=True)

    def load(chunk):
        return pltpu.make_async_copy(matrix.at[pl.ds(chunk * CHUNK, CHUNK)], stage.at[chunk % 2], stage_sem.at[chunk % 2])

    load(0).start()
    load(1).start()
    factors_here = pltpu.make_async_copy(factors, factor_ref, local_sem.at[3])
    factors_here.start()
    mixing[...] = jnp.zeros_like(mixing)
    mixing[0:size, 0:share] = v_ref[...]
    turned = mixing[:, 0:WIDE].T
    own[0:share, :] = turned[0:share, 0:LANES]
    near_rows, far_rows = turned[0 : share // 2, LANES:], turned[share // 2 : share, LANES:]
    own[share:, :] = jnp.where(left_lanes(near_rows.shape), near_rows, swap_halves(far_rows))
    enter(place, True)
    mail = Mail(send_sem, recv_sem)
    spread_v, spread_y = Spread(place, mail), Spread(place, mail)
    ring_v = RowRing(place, mail, own, row_v, local_sem.at[2])
    ring_y = RowRing(place, mail, share_sum, row_y, local_sem.at[4])
    rings_v, rings_y = ColumnRings(place, mail, col_v), ColumnRings(place, mail, col_y)
    mine = place.column_slot()
    todo = list(range(chunks))

    def convert(count):
        for _ in range(count):
            chunk = todo.pop(0)
            load(chunk).wait()
            top, rest = split(stage[chunk % 2])
            high[pl.ds(chunk * CHUNK, CHUNK), :] = top.astype(BF16)
            low[pl.ds(chunk * CHUNK, CHUNK), :] = rest.astype(BF16)
            if chunk + 2 < chunks:
                load(chunk + 2).start()

    spread_v.start(own, col_v.at[place.spread_slot()], col_v.at[mine], local_sem.at[0])
    ring_v.start()
    convert(3)
    spread_v.arrived()
    rings_v.start()
    ring_v.near()
    convert(2)
    rings_v.first_ring()
    convert(1)
    rings_v.second_ring(0)
    ring_v.far()
    convert(1)
    rings_v.first_ring_far()
    convert(1)
    rings_v.second_ring(-1)
    convert(1)
    rings_v.second_ring(1)
    convert(1)
    rings_v.second_ring(2)
    ring_v.end()
    for slot in range(8):
        unpack(row_v.at[slot], row_wide, slot * share)
    flat_v[...] = row_wide[...].T[0:size, :]
    gram = contract(flat_v[...], row_wide[...], 1, 0, HIGH) * 0.125
    grams_ref[2 * size : 3 * size, :] = gram[:, 0:LANES]
    grams_ref[3 * size : 4 * size, :] = gram[:, LANES:]
    rings_v.last()
    for slot in range(16):
        unpack_split(col_v.at[slot], right, slot * share)

    first, second, _, _ = spans(rows)
    near_up, near_down = place.at(y=1), place.at(y=-1)
    across = {y: mail.number() for y in (2, 1, -1, 0)}
    far_up, far_down, up_now, up_later, down_now, down_later = (mail.number() for _ in range(6))
    left = left_lanes((share // 2, LANES))

    def product(y):
        block = lax.rem(place.y + y + SIDE, SIDE)
        here = pl.ds(pl.multiple_of(block * 2 * share, 2 * share), 2 * share)
        top = jnp.dot(high[here, :], right[:, 0 : 3 * LANES], preferred_element_type=F32)
        rest = jnp.dot(low[here, :], right[:, LANES : 3 * LANES], preferred_element_type=F32)
        main = top[:, 0:LANES] + top[:, LANES : 2 * LANES] + rest[:, 0:LANES]
        tail = top[:, 2 * LANES :] + rest[:, LANES:]
        tail = tail + swap_halves(tail)
        wide_y[here, 0:LANES] = main
        wide_y[here, LANES:WIDE] = jnp.where(left_lanes(tail.shape), tail, 0.0)
        for core in range(2):
            slot = (y % SIDE) * 2 + core
            start = core * share
            partial[slot, 0:share, :] = main[start : start + share]
            upper, lower = tail[start : start + share // 2], tail[start + share // 2 : start + share]
            partial[slot, share:, :] = jnp.where(left, upper, lower)
        slot = (y % SIDE) * 2 + 1 - place.core
        mail.send(across[y], partial.at[slot], swap.at[y % SIDE], partner)

    def add_across(y):
        slot = y % SIDE
        mail.receive(across[y], swap.at[slot], partner)
        sums[slot, :, :] = partial[slot * 2 + place.core] + swap[slot]

    product(2)
    product(1)
    add_across(2)
    mail.send(far_up, sums.at[2, first], near.at[0, first], near_up)
    mail.send(far_down, sums.at[2, second], near.at[0, second], near_down)
    product(-1)
    add_across(1)
    mail.send(up_now, sums.at[1, second], near.at[1, second], near_up)
    product(0)
    add_across(-1)
    mail.send(down_now, sums.at[3, first], near.at[2, first], near_down)
    gram = contract(flat_v[...], wide_y[...], 1, 0, HIGH)
    grams_ref[0:size, :] = gram[:, 0:LANES]
    grams_ref[size : 2 * size, :] = gram[:, LANES:]

    half = grams_ref.shape[0] // 2
    part = half // SIDE
    cores = mail.number()
    mail.send(cores, grams_ref.at[pl.ds(pl.multiple_of((1 - place.core) * half, 8), half)], grams_swap, partner)

    def exchange(axis, source, landing):
        numbers = [mail.number() for _ in range(1, SIDE)]
        for step in range(1, SIDE):
            mail.send(numbers[step - 1], source(step), landing.at[step - 1], place.at(**{axis: step}))

        def arrived():
            for step in range(1, SIDE):
                mail.receive(numbers[step - 1], landing.at[step - 1], place.at(**{axis: -step}))
            return landing[0] + landing[1] + landing[2]

        return arrived

    def quarter(step):
        return pl.ds(pl.multiple_of(lax.rem(place.y + step, SIDE) * part, 8), part)

    mail.receive(far_up, near.at[0, first], near_down)
    sums[1, first, :] = sums[1, first, :] + near[0, first, :]
    mail.send(up_later, sums.at[1, first], near.at[1, first], near_up)
    mail.receive(far_down, near.at[0, second], near_up)
    sums[3, second, :] = sums[3, second, :] + near[0, second, :]
    mail.send(down_later, sums.at[3, second], near.at[2, second], near_down)
    add_across(0)
    mail.receive(cores, grams_swap, partner)
    core_half = pl.ds(pl.multiple_of(place.core * half, 8), half)
    grams_sum[pl.ds(0, half), :] = grams_ref[core_half, :] + grams_swap[...]
    over_y = exchange("y", lambda step: grams_sum.at[quarter(step)], grams_y)
    mail.receive(up_now, near.at[1, second], near_down)
    mail.receive(down_now, near.at[2, first], near_up)
    mail.receive(up_later, near.at[1, first], near_down)
    mail.receive(down_later, near.at[2, second], near_up)
    share_sum[...] = sums[0] + near[1] + near[2]

    spread_y.start(share_sum, col_y.at[place.spread_slot()], col_y.at[mine], local_sem.at[1])
    ring_y.start()
    grams_sum[pl.ds(half, part), :] = grams_sum[quarter(0), :] + over_y()
    over_x = exchange("x", lambda step: grams_sum.at[pl.ds(half, part)], grams_x)
    spread_y.arrived()
    rings_y.start()
    grams_sum[pl.ds(half + part, part), :] = grams_sum[pl.ds(half, part), :] + over_x()
    over_z = exchange("z", lambda step: grams_sum.at[pl.ds(half + part, part)], grams_z)

    def total_rows(y, other_core=False):
        core = 1 - place.core if other_core else place.core
        start = core * half + lax.rem(place.y + y + SIDE, SIDE) * part
        return total_ref.at[pl.ds(pl.multiple_of(start, 8), part)]

    back_y = [mail.number() for _ in range(1, SIDE)]
    back_core = [mail.number() for _ in range(SIDE)]
    ring_y.near()
    rings_y.first_ring()
    start = place.core * half + place.y * part
    total_ref[pl.ds(pl.multiple_of(start, 8), part), :] = grams_sum[pl.ds(half + part, part), :] + over_z()
    for step in range(1, SIDE):
        mail.send(back_y[step - 1], total_rows(0), total_rows(0), place.at(y=step))
    mail.send(back_core[0], total_rows(0), total_rows(0), partner)
    rings_y.second_ring(0)
    ring_y.far()
    rings_y.first_ring_far()
    rings_y.second_ring(-1)
    for step in range(1, SIDE):
        mail.receive(back_y[step - 1], total_rows(-step), place.at(y=-step))
        mail.send(back_core[step], total_rows(-step), total_rows(-step), partner)
    rings_y.second_ring(1)
    for step in range(SIDE):
        mail.receive(back_core[step], total_rows(-step, True), partner)
    factors_here.wait()

    begin, step = coefficient_steps(panels, width, total_ref, factor_ref, of_y, of_v, of_w)

    def mix():
        mixing[...] = jnp.zeros_like(mixing)
        of_d, of_c = of_w[:, WIDE : 2 * WIDE], of_w[:, 2 * WIDE :]
        mixing[0:size, 0:WIDE] = of_d
        mixing[:, 0:WIDE] = mixing[:, 0:WIDE] + mixing[:, 0:WIDE].T
        mixing[0:size, WIDE:] = of_c

    def store_left(value, start, lane, low_lane):
        left = left_lanes((share, LANES))
        for at in range(2):
            top, rest = split(value[:, at * LANES : (at + 1) * LANES])
            if at:
                top = jnp.where(left, top, swap_halves(top))
                rest = jnp.where(left, rest, swap_halves(rest))
            here = pl.ds(start, share)
            low_here = slice(low_lane + at * LANES, low_lane + (at + 1) * LANES)
            left_low[here, low_here] = rest.astype(BF16)
            if not at:
                left_high[here, lane : lane + LANES] = top.astype(BF16)
            left_high[here, lane + (at + 1) * LANES : lane + (at + 2) * LANES] = top.astype(BF16)

    def left_rows(slot):
        unpack(row_y.at[slot], share_y, 0)
        here = pl.ds(slot * share, share)
        of_right_v = contract(row_wide[here, :], mixing[:, 0:WIDE], 1, 0, HIGH)
        of_right_v = of_right_v + contract(share_y[...], mixing[:, WIDE:], 1, 1, HIGH)
        of_right_y = contract(row_wide[here, :], mixing[:, WIDE:], 1, 0, HIGH)
        store_left(of_right_v, slot * share, 0, 0)
        store_left(of_right_y, slot * share, 3 * LANES, 2 * LANES)

    begin()
    step(0)
    rings_y.second_ring(2)
    step(1)
    step(2)
    step(3)
    step(4)
    step(5)
    mix()
    unpack(own, share_v, 0)
    unpack(share_sum, share_y, 0)
    w_ref[...] = contract(of_w[:, WIDE : 2 * WIDE], share_v[...], 1, 1, HIGH)
    w_ref[...] = w_ref[...] + contract(of_w[:, 2 * WIDE :], share_y[...], 1, 1, HIGH)
    ring_y.end()
    for slot in range(8):
        left_rows(slot)
    rings_y.last()
    for slot in range(16):
        unpack_split(col_y.at[slot], right, slot * share, 3 * LANES)
    spread_v.finish()
    spread_y.finish()
    mail.finish()


def in_vmem(count):
    return [pl.BlockSpec(memory_space=pltpu.VMEM)] * count


def factors_call(v, matrix, factors):
    size, share = v.shape
    rows, lanes = share + share // 2, LANES
    height, length = matrix.shape
    panels, width, _ = factors.shape
    grams = 4 * size
    part = grams // 8
    return pl.pallas_call(
        functools.partial(factors_kernel, panels, width),
        out_shape=(
            jax.ShapeDtypeStruct((length, 6 * lanes), BF16),
            jax.ShapeDtypeStruct((height, 6 * lanes), BF16),
            jax.ShapeDtypeStruct((height, 4 * lanes), BF16),
            jax.ShapeDtypeStruct((size, share), F32),
        ),
        in_specs=in_vmem(1) + [pl.BlockSpec(memory_space=pl.ANY)] * 2,
        out_specs=in_vmem(4),
        scratch_shapes=[
            pltpu.VMEM((2, CHUNK, length), F32),
            pltpu.VMEM((height, length), BF16),
            pltpu.VMEM((height, length), BF16),
            pltpu.VMEM((8, rows, lanes), F32),
            pltpu.VMEM((8, rows, lanes), F32),
            pltpu.VMEM((16, rows, lanes), F32),
            pltpu.VMEM((16, rows, lanes), F32),
            pltpu.VMEM((height, WIDE), F32),
            pltpu.VMEM((size, height), F32),
            pltpu.VMEM((height, WIDE), F32),
            pltpu.VMEM((8, rows, lanes), F32),
            pltpu.VMEM((SIDE, rows, lanes), F32),
            pltpu.VMEM((SIDE, rows, lanes), F32),
            pltpu.VMEM((3, rows, lanes), F32),
            pltpu.VMEM((rows, lanes), F32),
            pltpu.VMEM((rows, lanes), F32),
            pltpu.VMEM(factors.shape, F32),
            pltpu.VMEM((grams, lanes), F32),
            pltpu.VMEM((grams, lanes), F32),
            pltpu.VMEM((SIDE * part, lanes), F32),
            pltpu.VMEM((6 * part, lanes), F32),
            pltpu.VMEM((3, part, lanes), F32),
            pltpu.VMEM((3, part, lanes), F32),
            pltpu.VMEM((3, part, lanes), F32),
            pltpu.VMEM((size, 3 * WIDE), F32),
            pltpu.VMEM((size, 3 * WIDE), F32),
            pltpu.VMEM((size, 3 * WIDE), F32),
            pltpu.VMEM((WIDE, 2 * WIDE), F32),
            pltpu.VMEM((share, WIDE), F32),
            pltpu.VMEM((share, WIDE), F32),
            pltpu.SemaphoreType.DMA((192,)),
            pltpu.SemaphoreType.DMA((192,)),
            pltpu.SemaphoreType.DMA((5,)),
            pltpu.SemaphoreType.DMA((2,)),
        ],
        compiler_params=pltpu.CompilerParams(collective_id=0, has_side_effects=True, vmem_limit_bytes=42 * 1024 * 1024),
        cost_estimate=pl.CostEstimate(flops=50_000_000_000, bytes_accessed=100_000_000, transcendentals=0),
        name="factors",
    )(v, matrix, factors)


TILE = 256


def update_kernel(matrix_ref, right_ref, high_ref, low_ref, w_in, out_ref, w_out):
    right = right_ref[...]
    change = contract(high_ref[...], right, 1, 1, None)
    low_v, low_y = low_ref[:, 0 : 2 * LANES], low_ref[:, 2 * LANES :]
    change = change + contract(low_v, right[:, LANES : 3 * LANES], 1, 1, None)
    change = change + contract(low_y, right[:, 4 * LANES :], 1, 1, None)
    out_ref[...] = matrix_ref[...] - change
    w_out[...] = w_in[...]


def update_call(matrix, right, left_high, left_low, w):
    height, length = matrix.shape

    def whole(array):
        return pl.BlockSpec(array.shape, lambda tile: (0, 0), pipeline_mode=pl.Buffered(1))

    return pl.pallas_call(
        update_kernel,
        grid=(length // TILE,),
        out_shape=(jax.ShapeDtypeStruct(matrix.shape, F32), jax.ShapeDtypeStruct(w.shape, F32)),
        in_specs=[
            pl.BlockSpec((height, TILE), lambda tile: (0, tile)),
            pl.BlockSpec((TILE, right.shape[1]), lambda tile: (tile, 0)),
            whole(left_high),
            whole(left_low),
            whole(w),
        ],
        out_specs=[pl.BlockSpec((height, TILE), lambda tile: (0, tile)), pl.BlockSpec(w.shape, lambda tile: (0, 0))],
        compiler_params=pltpu.CompilerParams(dimension_semantics=("arbitrary",), vmem_limit_bytes=14 * 1024 * 1024),
        name="update",
    )(matrix, right, left_high, left_low, w)


def per_device(trailing, v_panels, t_panels):
    panels, width, share = v_panels.shape
    size = panels * width
    v = v_panels.reshape(size, share)
    right, left_high, left_low, w = factors_call(v, trailing, t_panels)
    matrix, w = update_call(trailing, right, left_high, left_low, w)
    return (matrix, w.reshape(panels, width, share))


def solution(mesh):
    return jax.shard_map(
        per_device,
        mesh=mesh,
        in_specs=(P("pr", "pc"), P(None, None, ("pr", "pc")), P()),
        out_specs=(P("pr", "pc"), P(None, None, ("pr", "pc"))),
        check_vma=False,
    )
```

```python
import functools

import jax
import jax.numpy as jnp
from jax import lax
from jax.experimental import pallas as pl
from jax.experimental.pallas import tpu as pltpu
from jax.sharding import PartitionSpec as P

HIGHEST = lax.Precision.HIGHEST
MESH = pl.DeviceIdType.MESH
SIDE = 4


class Place:
    def __init__(self):
        pr, pc = lax.axis_index("pr"), lax.axis_index("pc")
        self.x, self.z = lax.rem(pr, SIDE), lax.div(pr, SIDE)
        self.y, self.core = lax.div(pc, 2), lax.rem(pc, 2)

    def at(self, x=0, y=0, z=0, other_core=False):
        far_x = lax.rem(self.x + x + SIDE, SIDE)
        far_y = lax.rem(self.y + y + SIDE, SIDE)
        far_z = lax.rem(self.z + z + SIDE, SIDE)
        core = 1 - self.core if other_core else self.core
        return far_z * SIDE + far_x, far_y * 2 + core

    def spread_to(self):
        block = lax.div(self.x, 2)
        keep = jnp.where(self.core == block, 1, 0)
        far_x = keep * self.x + (1 - keep) * (SIDE - 1 - self.x)
        return lax.rem(self.y + self.z, SIDE) * SIDE + far_x, self.z * 2 + block

    def spread_slot(self):
        block = lax.div(self.x, 2)
        return (self.x - 2 * block) * 8 + 2 * self.y + self.core

    def spread_from(self):
        keep = jnp.where(lax.div(self.x, 2) == self.core, 1, 0)
        far_x = keep * self.x + (1 - keep) * (SIDE - 1 - self.x)
        core = keep * self.core + (1 - keep) * (1 - self.core)
        return self.y * SIDE + far_x, lax.rem(self.z - self.y + SIDE, SIDE) * 2 + core

    def column_slot(self, x=0, z=0):
        far_x = lax.rem(self.x + x + SIDE, SIDE)
        far_z = lax.rem(self.z + z + SIDE, SIDE)
        keep = jnp.where(lax.div(far_x, 2) == self.core, 1, 0)
        from_x = keep * far_x + (1 - keep) * (SIDE - 1 - far_x)
        core = keep * self.core + (1 - keep) * (1 - self.core)
        return (from_x - 2 * self.core) * 8 + 2 * lax.rem(far_z - self.y + SIDE, SIDE) + core

    def row_slot(self, y=0, other_core=False):
        core = 1 - self.core if other_core else self.core
        return lax.rem(self.y + y + SIDE, SIDE) * 2 + core


class Mail:
    def __init__(self, send_sem, recv_sem):
        self.send_sem, self.recv_sem = send_sem, recv_sem
        self.count, self.sent = 0, []

    def number(self):
        self.count += 1
        return self.count - 1

    def copy(self, number, source, target, device):
        return pltpu.make_async_remote_copy(
            src_ref=source,
            dst_ref=target,
            send_sem=self.send_sem.at[number],
            recv_sem=self.recv_sem.at[number],
            device_id=device,
            device_id_type=MESH,
        )

    def send(self, number, source, target, device):
        copy = self.copy(number, source, target, device)
        copy.start()
        self.sent.append(copy)

    def receive(self, number, landed, device):
        self.copy(number, landed, landed, device).wait_recv()

    def finish(self):
        for copy in self.sent:
            copy.wait_send()


def is_here(device, place):
    pr, pc = place.at()
    return jnp.logical_and(device[0] == pr, device[1] == pc)


def spans(rows):
    half = rows // 2
    cut = -(-half // 16) * 8
    first, second = pl.ds(0, half), pl.ds(half, half)
    return (
        first,
        second,
        (pl.ds(0, cut), pl.ds(cut, half - cut)),
        (pl.ds(half, cut), pl.ds(half + cut, half - cut)),
    )


class Spread:
    def __init__(self, place, mail, back=False):
        self.mail, self.number = mail, mail.number()
        self.target = place.spread_from() if back else place.spread_to()
        self.source = place.spread_to() if back else place.spread_from()
        self.stays = is_here(self.target, place)

    def start(self, own, landing, landed, local_sem):
        self.own, self.landed = own, landed
        self.local = pltpu.make_async_copy(own, landed, local_sem)
        self.remote = self.mail.copy(self.number, own, landing, self.target)

        @pl.when(jnp.logical_not(self.stays))
        def _():
            self.remote.start()

        @pl.when(self.stays)
        def _():
            self.local.start()

    def arrived(self):
        @pl.when(jnp.logical_not(self.stays))
        def _():
            self.mail.copy(self.number, self.own, self.landed, self.source).wait_recv()

        @pl.when(self.stays)
        def _():
            self.local.wait()

    def finish(self):
        @pl.when(jnp.logical_not(self.stays))
        def _():
            self.remote.wait_send()


class RowRing:
    def __init__(self, place, mail, own, row, local_sem):
        self.place, self.mail, self.own, self.row = place, mail, own, row
        self.first, self.second, _, _ = spans(own.shape[0])
        self.up, self.down, self.up_on, self.down_on = (mail.number() for _ in range(4))
        self.cross = [mail.number() for _ in range(4)]
        self.partner = place.at(other_core=True)
        self.near_up, self.near_down = place.at(y=1), place.at(y=-1)
        self.keep = pltpu.make_async_copy(own, row.at[place.row_slot()], local_sem)

    def start(self):
        here = self.row.at[self.place.row_slot()]
        self.keep.start()
        self.mail.send(self.up, self.own, here, self.near_up)
        self.mail.send(self.down, self.own, here, self.near_down)
        self.mail.send(self.cross[0], self.own, here, self.partner)

    def near(self):
        mail, row = self.mail, self.row
        below, above = self.place.row_slot(y=-1), self.place.row_slot(y=1)
        mail.receive(self.up, row.at[below], self.near_down)
        mail.send(self.up_on, row.at[below, self.first], row.at[below, self.first], self.near_up)
        mail.send(self.cross[1], row.at[below], row.at[below], self.partner)
        mail.receive(self.down, row.at[above], self.near_up)
        mail.send(self.down_on, row.at[above, self.second], row.at[above, self.second], self.near_down)
        mail.send(self.cross[2], row.at[above], row.at[above], self.partner)

    def far(self):
        mail, row = self.mail, self.row
        far = self.place.row_slot(y=2)
        mail.receive(self.up_on, row.at[far, self.first], self.near_down)
        mail.receive(self.down_on, row.at[far, self.second], self.near_up)
        mail.send(self.cross[3], row.at[far], row.at[far], self.partner)

    def end(self):
        for number, y in ((0, 0), (1, -1), (2, 1), (3, 2)):
            landed = self.row.at[self.place.row_slot(y=y, other_core=True)]
            self.mail.receive(self.cross[number], landed, self.partner)
        self.keep.wait()


OTHER = {"x": "z", "z": "x"}


class ColumnRings:
    def __init__(self, place, mail, col):
        self.place, self.mail, self.col, self.numbers = place, mail, col, {}
        first, second, first_cut, second_cut = spans(col.shape[1])
        self.halves = {"x": (first, first_cut), "z": (second, second_cut)}

    def number(self, *key):
        if key not in self.numbers:
            self.numbers[key] = self.mail.number()
        return self.numbers[key]

    def ref(self, axis, along, across, span):
        x, z = (along, across) if axis == "x" else (across, along)
        return self.col.at[self.place.column_slot(x=x, z=z), span]

    def to(self, axis, step):
        return self.place.at(**{axis: step})

    def push(self, axis, step, half, across, span, along=0):
        ref = self.ref(axis, along, across, span)
        self.mail.send(self.number(axis, step, half, across, along), ref, ref, self.to(axis, step))

    def pull(self, axis, step, half, across, span, along=0):
        ref = self.ref(axis, along - step, across, span)
        self.mail.receive(self.number(axis, step, half, across, along), ref, self.to(axis, -step))

    def pass_on(self, axis, half, across):
        span = self.halves[half][0]
        for step in (1, -1):
            self.push(axis, step, half, across, span)
        if half == axis:
            ref = self.ref(axis, 0, across, span)
            self.mail.send(self.number(axis, "far", half, across), ref, ref, self.to(axis, 2))

    def take(self, axis, step, half, across):
        self.pull(axis, step, half, across, self.halves[half][0])
        if half != axis:
            self.push(axis, step, half, across, self.halves[half][1][0 if step == 1 else 1], along=-step)

    def take_far(self, axis, half, across):
        if half == axis:
            ref = self.ref(axis, 2, across, self.halves[half][0])
            self.mail.receive(self.number(axis, "far", half, across), ref, self.to(axis, 2))
        else:
            for step, part in ((1, 0), (-1, 1)):
                self.pull(axis, step, half, across, self.halves[half][1][part], along=-step)

    def start(self):
        for axis in ("x", "z"):
            self.pass_on(axis, axis, 0)
        for axis in ("x", "z"):
            self.pass_on(axis, OTHER[axis], 0)

    def first_ring(self):
        for step in (1, -1):
            for axis in ("x", "z"):
                self.take(axis, step, axis, 0)
                self.pass_on(OTHER[axis], axis, -step)

    def first_ring_far(self):
        for axis in ("x", "z"):
            self.take_far(axis, axis, 0)
            self.pass_on(OTHER[axis], axis, 2)

    def second_ring(self, across):
        for step in (1, -1):
            for axis in ("x", "z"):
                self.take(axis, step, OTHER[axis], across)

    def last(self):
        for across in (0, -1, 1, 2):
            for axis in ("x", "z"):
                self.take_far(axis, OTHER[axis], across)


def greet(place, far):
    barrier = pltpu.get_barrier_semaphore()
    near = [place.at(x=1), place.at(x=-1), place.at(z=1), place.at(z=-1), place.at(y=1), place.at(y=-1)]
    near.append(place.at(other_core=True))
    if far:
        near += [place.at(x=2), place.at(y=2), place.at(z=2)]
    target, source = place.spread_to(), place.spread_from()
    moves = jnp.logical_not(is_here(target, place))
    for device in near:
        pl.semaphore_signal(barrier, inc=1, device_id=device, device_id_type=MESH)

    @pl.when(moves)
    def _():
        for device in (target, source):
            pl.semaphore_signal(barrier, inc=1, device_id=device, device_id_type=MESH)

    return len(near) + jnp.where(moves, 2, 0)


HIGH = lax.Precision.HIGH
BF16 = jnp.bfloat16
F32 = jnp.float32
LANES = 128
WIDE = 2 * LANES


def contract(left_side, right_side, left_dim, right_dim, precision=HIGHEST):
    return lax.dot_general(
        left_side,
        right_side,
        (((left_dim,), (right_dim,)), ((), ())),
        precision=precision,
        preferred_element_type=F32,
    )


def split(value):
    high = value.astype(BF16).astype(F32)
    return high, value - high


def left_lanes(shape):
    return lax.broadcasted_iota(jnp.int32, shape, len(shape) - 1) < LANES // 2


def swap_halves(value):
    return pltpu.roll(value, LANES // 2, 1)


def unpack(packed, wide, start):
    rows = packed.shape[0] // 3
    tail = packed[pl.ds(2 * rows, rows), :]
    left = left_lanes(tail.shape)
    wide[pl.ds(start, 2 * rows), 0:LANES] = packed[pl.ds(0, 2 * rows), :]
    wide[pl.ds(start, rows), LANES:WIDE] = jnp.where(left, tail, 0.0)
    wide[pl.ds(start + rows, rows), LANES:WIDE] = jnp.where(left, swap_halves(tail), 0.0)


def unpack_split(packed, parts, start, lane=0):
    rows = packed.shape[0] // 3
    high, low = split(packed[pl.ds(0, 2 * rows), :])
    parts[pl.ds(start, 2 * rows), lane : lane + LANES] = low.astype(BF16)
    parts[pl.ds(start, 2 * rows), lane + LANES : lane + 2 * LANES] = high.astype(BF16)
    high, low = split(packed[pl.ds(2 * rows, rows), :])
    left = left_lanes(high.shape)
    ends = slice(lane + 2 * LANES, lane + 3 * LANES)
    parts[pl.ds(start, rows), ends] = jnp.where(left, high, swap_halves(low)).astype(BF16)
    parts[pl.ds(start + rows, rows), ends] = jnp.where(left, swap_halves(high), low).astype(BF16)


def coefficient_steps(panels, width, total_ref, factor_ref, of_y, of_v, of_w):
    size = panels * width

    def begin():
        rows = lax.broadcasted_iota(jnp.int32, (size, WIDE), 0)
        cols = lax.broadcasted_iota(jnp.int32, (size, WIDE), 1)
        eye = jnp.where(rows == cols, 1.0, 0.0)
        zero = jnp.zeros((size, WIDE), F32)
        for ref, first, at in ((of_y, 0, 2), (of_v, 2 * size, 1)):
            ref[:, 0:LANES] = total_ref[pl.ds(first, size), :]
            ref[:, LANES:WIDE] = total_ref[pl.ds(first + size, size), :]
            ref[:, WIDE * at : WIDE * (at + 1)] = eye
            ref[:, WIDE * (3 - at) : WIDE * (4 - at)] = zero

    def step(panel):
        start = panel * width
        here = slice(start, start + width)
        of_x = of_y[here, :]
        if panel:
            before = slice(0, start)
            of_x = of_x - contract(of_w[before, here], of_v[before, :], 0, 0)
            of_x = of_x - contract(of_v[before, here], of_w[before, :], 0, 0)
        factor = factor_ref[panel]
        scaled = contract(factor, of_x, 0, 0)
        middle = contract(scaled[:, here], factor, 1, 0)
        of_w[here, :] = scaled - 0.5 * contract(middle, of_v[here, :], 1, 0)

    return begin, step


CHUNK = 128
NEAR = [(x, z) for x in (0, 1, -1) for z in (0, 1, -1)]
FAR = [(x, z) for x in (0, 1, -1, 2) for z in (0, 1, -1, 2) if 2 in (x, z)]


def factors_kernel(
    panels,
    width,
    v_ref,
    matrix,
    factors,
    right,
    left_high,
    left_low,
    w_ref,
    stage,
    high,
    low,
    row_v,
    row_y,
    col_v,
    col_y,
    row_wide,
    flat_v,
    wide_y,
    partial,
    swap,
    sums,
    near,
    share_sum,
    own,
    v_own,
    factor_ref,
    grams_ref,
    total_ref,
    grams_swap,
    grams_sum,
    grams_y,
    grams_x,
    grams_z,
    of_y,
    of_v,
    of_w,
    mixing,
    share_v,
    share_y,
    send_sem,
    recv_sem,
    local_sem,
    stage_sem,
):
    place = Place()
    rows = own.shape[0]
    size = panels * width
    share = v_ref.shape[1]
    chunks = matrix.shape[0] // CHUNK
    partner = place.at(other_core=True)

    def load(chunk):
        return pltpu.make_async_copy(matrix.at[pl.ds(chunk * CHUNK, CHUNK)], stage.at[chunk % 2], stage_sem.at[chunk % 2])

    v_here = pltpu.make_async_copy(v_ref, v_own, local_sem.at[0])
    v_here.start()
    factors_here = pltpu.make_async_copy(factors, factor_ref, local_sem.at[3])
    factors_here.start()
    load(0).start()
    load(1).start()
    greeted = greet(place, True)
    mixing[...] = jnp.zeros_like(mixing)
    v_here.wait()
    mixing[0:size, 0:share] = v_own[...]
    turned = mixing[:, 0:WIDE].T
    own[0:share, :] = turned[0:share, 0:LANES]
    near_rows, far_rows = turned[0 : share // 2, LANES:], turned[share // 2 : share, LANES:]
    own[share:, :] = jnp.where(left_lanes(near_rows.shape), near_rows, swap_halves(far_rows))
    pl.semaphore_wait(pltpu.get_barrier_semaphore(), greeted)
    mail = Mail(send_sem, recv_sem)
    spread_v, spread_y = Spread(place, mail), Spread(place, mail)
    ring_v = RowRing(place, mail, own, row_v, local_sem.at[2])
    ring_y = RowRing(place, mail, share_sum, row_y, local_sem.at[4])
    rings_v, rings_y = ColumnRings(place, mail, col_v), ColumnRings(place, mail, col_y)
    mine = place.column_slot()
    todo = list(range(chunks))

    def convert(count):
        for _ in range(count):
            chunk = todo.pop(0)
            load(chunk).wait()
            top, rest = split(stage[chunk % 2])
            high[pl.ds(chunk * CHUNK, CHUNK), :] = top.astype(BF16)
            low[pl.ds(chunk * CHUNK, CHUNK), :] = rest.astype(BF16)
            if chunk + 2 < chunks:
                load(chunk + 2).start()

    def unpack_columns(col, lane, chips):
        for x, z in chips:
            slot = place.column_slot(x=x, z=z)
            unpack_split(col.at[slot], right, pl.multiple_of(slot * share, 32), lane)

    spread_v.start(own, col_v.at[place.spread_slot()], col_v.at[mine], local_sem.at[0])
    convert(4)
    spread_v.arrived()
    rings_v.start()
    ring_v.start()
    convert(2)
    rings_v.first_ring()
    ring_v.near()
    convert(1)
    rings_v.second_ring(0)
    convert(1)
    rings_v.first_ring_far()
    ring_v.far()
    convert(1)
    rings_v.second_ring(-1)
    convert(1)
    rings_v.second_ring(1)
    rings_v.second_ring(2)
    ring_v.end()
    for slot in range(8):
        unpack(row_v.at[slot], row_wide, slot * share)
    flat_v[...] = row_wide[...].T[0:size, :]
    gram = contract(flat_v[...], row_wide[...], 1, 0, HIGH) * 0.125
    grams_ref[2 * size : 3 * size, :] = gram[:, 0:LANES]
    grams_ref[3 * size : 4 * size, :] = gram[:, LANES:]
    unpack_columns(col_v, 0, NEAR)
    rings_v.last()
    unpack_columns(col_v, 0, FAR)

    first, second, _, _ = spans(rows)
    near_up, near_down = place.at(y=1), place.at(y=-1)
    across = {y: mail.number() for y in (2, 1, -1, 0)}
    far_up, far_down, up_now, up_later, down_now, down_later = (mail.number() for _ in range(6))
    left = left_lanes((share // 2, LANES))

    def product(y):
        block = lax.rem(place.y + y + SIDE, SIDE)
        here = pl.ds(pl.multiple_of(block * 2 * share, 2 * share), 2 * share)
        top = jnp.dot(high[here, :], right[:, 0 : 3 * LANES], preferred_element_type=F32)
        rest = jnp.dot(low[here, :], right[:, LANES : 3 * LANES], preferred_element_type=F32)
        main = top[:, 0:LANES] + top[:, LANES : 2 * LANES] + rest[:, 0:LANES]
        tail = top[:, 2 * LANES :] + rest[:, LANES:]
        tail = tail + swap_halves(tail)
        wide_y[here, 0:LANES] = main
        wide_y[here, LANES:WIDE] = jnp.where(left_lanes(tail.shape), tail, 0.0)
        for core in range(2):
            slot = (y % SIDE) * 2 + core
            start = core * share
            partial[slot, 0:share, :] = main[start : start + share]
            upper, lower = tail[start : start + share // 2], tail[start + share // 2 : start + share]
            partial[slot, share:, :] = jnp.where(left, upper, lower)
        slot = (y % SIDE) * 2 + 1 - place.core
        mail.send(across[y], partial.at[slot], swap.at[y % SIDE], partner)

    def add_across(y):
        slot = y % SIDE
        mail.receive(across[y], swap.at[slot], partner)
        sums[slot, :, :] = partial[slot * 2 + place.core] + swap[slot]

    product(2)
    product(1)
    add_across(2)
    mail.send(far_up, sums.at[2, first], near.at[0, first], near_up)
    mail.send(far_down, sums.at[2, second], near.at[0, second], near_down)
    product(-1)
    add_across(1)
    mail.send(up_now, sums.at[1, second], near.at[1, second], near_up)
    product(0)
    add_across(-1)
    mail.send(down_now, sums.at[3, first], near.at[2, first], near_down)
    gram = contract(flat_v[...], wide_y[...], 1, 0, HIGH)
    grams_ref[0:size, :] = gram[:, 0:LANES]
    grams_ref[size : 2 * size, :] = gram[:, LANES:]

    half = grams_ref.shape[0] // 2
    part = half // SIDE
    cores = mail.number()
    mail.send(cores, grams_ref.at[pl.ds(pl.multiple_of((1 - place.core) * half, 8), half)], grams_swap, partner)

    def exchange(axis, source, landing):
        numbers = [mail.number() for _ in range(1, SIDE)]
        for step in range(1, SIDE):
            mail.send(numbers[step - 1], source(step), landing.at[step - 1], place.at(**{axis: step}))

        def arrived():
            for step in range(1, SIDE):
                mail.receive(numbers[step - 1], landing.at[step - 1], place.at(**{axis: -step}))
            return landing[0] + landing[1] + landing[2]

        return arrived

    def quarter(step):
        return pl.ds(pl.multiple_of(lax.rem(place.y + step, SIDE) * part, 8), part)

    mail.receive(far_up, near.at[0, first], near_down)
    sums[1, first, :] = sums[1, first, :] + near[0, first, :]
    mail.send(up_later, sums.at[1, first], near.at[1, first], near_up)
    mail.receive(far_down, near.at[0, second], near_up)
    sums[3, second, :] = sums[3, second, :] + near[0, second, :]
    mail.send(down_later, sums.at[3, second], near.at[2, second], near_down)
    add_across(0)
    mail.receive(cores, grams_swap, partner)
    core_half = pl.ds(pl.multiple_of(place.core * half, 8), half)
    grams_sum[pl.ds(0, half), :] = grams_ref[core_half, :] + grams_swap[...]
    over_y = exchange("y", lambda step: grams_sum.at[quarter(step)], grams_y)
    mail.receive(up_now, near.at[1, second], near_down)
    mail.receive(down_now, near.at[2, first], near_up)
    mail.receive(up_later, near.at[1, first], near_down)
    mail.receive(down_later, near.at[2, second], near_up)
    share_sum[...] = sums[0] + near[1] + near[2]

    spread_y.start(share_sum, col_y.at[place.spread_slot()], col_y.at[mine], local_sem.at[1])
    grams_sum[pl.ds(half, part), :] = grams_sum[quarter(0), :] + over_y()
    over_x = exchange("x", lambda step: grams_sum.at[pl.ds(half, part)], grams_x)
    spread_y.arrived()
    rings_y.start()
    ring_y.start()
    grams_sum[pl.ds(half + part, part), :] = grams_sum[pl.ds(half, part), :] + over_x()
    over_z = exchange("z", lambda step: grams_sum.at[pl.ds(half + part, part)], grams_z)

    def total_rows(y, other_core=False):
        core = 1 - place.core if other_core else place.core
        start = core * half + lax.rem(place.y + y + SIDE, SIDE) * part
        return total_ref.at[pl.ds(pl.multiple_of(start, 8), part)]

    back_y = [mail.number() for _ in range(1, SIDE)]
    back_core = [mail.number() for _ in range(SIDE)]
    rings_y.first_ring()
    ring_y.near()
    start = place.core * half + place.y * part
    total_ref[pl.ds(pl.multiple_of(start, 8), part), :] = grams_sum[pl.ds(half + part, part), :] + over_z()
    for step in range(1, SIDE):
        mail.send(back_y[step - 1], total_rows(0), total_rows(0), place.at(y=step))
    mail.send(back_core[0], total_rows(0), total_rows(0), partner)
    rings_y.second_ring(0)
    rings_y.first_ring_far()
    ring_y.far()
    rings_y.second_ring(-1)
    for step in range(1, SIDE):
        mail.receive(back_y[step - 1], total_rows(-step), place.at(y=-step))
        mail.send(back_core[step], total_rows(-step), total_rows(-step), partner)
    rings_y.second_ring(1)
    for step in range(SIDE):
        mail.receive(back_core[step], total_rows(-step, True), partner)
    factors_here.wait()

    begin, step = coefficient_steps(panels, width, total_ref, factor_ref, of_y, of_v, of_w)

    def mix():
        mixing[...] = jnp.zeros_like(mixing)
        of_d, of_c = of_w[:, WIDE : 2 * WIDE], of_w[:, 2 * WIDE :]
        mixing[0:size, 0:WIDE] = of_d
        mixing[:, 0:WIDE] = mixing[:, 0:WIDE] + mixing[:, 0:WIDE].T
        mixing[0:size, WIDE:] = of_c

    def store_left(value, start, lane, low_lane):
        left = left_lanes((share, LANES))
        for at in range(2):
            top, rest = split(value[:, at * LANES : (at + 1) * LANES])
            if at:
                top = jnp.where(left, top, swap_halves(top))
                rest = jnp.where(left, rest, swap_halves(rest))
            here = pl.ds(start, share)
            low_here = slice(low_lane + at * LANES, low_lane + (at + 1) * LANES)
            left_low[here, low_here] = rest.astype(BF16)
            if not at:
                left_high[here, lane : lane + LANES] = top.astype(BF16)
            left_high[here, lane + (at + 1) * LANES : lane + (at + 2) * LANES] = top.astype(BF16)

    def left_rows(slot):
        unpack(row_y.at[slot], share_y, 0)
        here = pl.ds(slot * share, share)
        of_right_v = contract(row_wide[here, :], mixing[:, 0:WIDE], 1, 0, HIGH)
        of_right_v = of_right_v + contract(share_y[...], mixing[:, WIDE:], 1, 1, HIGH)
        of_right_y = contract(row_wide[here, :], mixing[:, WIDE:], 1, 0, HIGH)
        store_left(of_right_v, slot * share, 0, 0)
        store_left(of_right_y, slot * share, 3 * LANES, 2 * LANES)

    begin()
    step(0)
    rings_y.second_ring(2)
    step(1)
    step(2)
    step(3)
    step(4)
    step(5)
    mix()
    unpack(own, share_v, 0)
    unpack(share_sum, share_y, 0)
    w_ref[...] = contract(of_w[:, WIDE : 2 * WIDE], share_v[...], 1, 1, HIGH)
    w_ref[...] = w_ref[...] + contract(of_w[:, 2 * WIDE :], share_y[...], 1, 1, HIGH)
    ring_y.end()
    for slot in range(8):
        left_rows(slot)
    unpack_columns(col_y, 3 * LANES, NEAR)
    rings_y.last()
    unpack_columns(col_y, 3 * LANES, FAR)
    spread_v.finish()
    spread_y.finish()
    mail.finish()


def in_vmem(count):
    return [pl.BlockSpec(memory_space=pltpu.VMEM)] * count


def factors_call(v, matrix, factors):
    size, share = v.shape
    rows, lanes = share + share // 2, LANES
    height, length = matrix.shape
    panels, width, _ = factors.shape
    grams = 4 * size
    part = grams // 8
    return pl.pallas_call(
        functools.partial(factors_kernel, panels, width),
        out_shape=(
            jax.ShapeDtypeStruct((length, 6 * lanes), BF16),
            jax.ShapeDtypeStruct((height, 6 * lanes), BF16),
            jax.ShapeDtypeStruct((height, 4 * lanes), BF16),
            jax.ShapeDtypeStruct((size, share), F32),
        ),
        in_specs=[pl.BlockSpec(memory_space=pltpu.HBM)] * 3,
        out_specs=in_vmem(4),
        scratch_shapes=[
            pltpu.VMEM((2, CHUNK, length), F32),
            pltpu.VMEM((height, length), BF16),
            pltpu.VMEM((height, length), BF16),
            pltpu.VMEM((8, rows, lanes), F32),
            pltpu.VMEM((8, rows, lanes), F32),
            pltpu.VMEM((16, rows, lanes), F32),
            pltpu.VMEM((16, rows, lanes), F32),
            pltpu.VMEM((height, WIDE), F32),
            pltpu.VMEM((size, height), F32),
            pltpu.VMEM((height, WIDE), F32),
            pltpu.VMEM((8, rows, lanes), F32),
            pltpu.VMEM((SIDE, rows, lanes), F32),
            pltpu.VMEM((SIDE, rows, lanes), F32),
            pltpu.VMEM((3, rows, lanes), F32),
            pltpu.VMEM((rows, lanes), F32),
            pltpu.VMEM((rows, lanes), F32),
            pltpu.VMEM((size, share), F32),
            pltpu.VMEM(factors.shape, F32),
            pltpu.VMEM((grams, lanes), F32),
            pltpu.VMEM((grams, lanes), F32),
            pltpu.VMEM((SIDE * part, lanes), F32),
            pltpu.VMEM((6 * part, lanes), F32),
            pltpu.VMEM((3, part, lanes), F32),
            pltpu.VMEM((3, part, lanes), F32),
            pltpu.VMEM((3, part, lanes), F32),
            pltpu.VMEM((size, 3 * WIDE), F32),
            pltpu.VMEM((size, 3 * WIDE), F32),
            pltpu.VMEM((size, 3 * WIDE), F32),
            pltpu.VMEM((WIDE, 2 * WIDE), F32),
            pltpu.VMEM((share, WIDE), F32),
            pltpu.VMEM((share, WIDE), F32),
            pltpu.SemaphoreType.DMA((192,)),
            pltpu.SemaphoreType.DMA((192,)),
            pltpu.SemaphoreType.DMA((5,)),
            pltpu.SemaphoreType.DMA((2,)),
        ],
        compiler_params=pltpu.CompilerParams(collective_id=0, has_side_effects=True, vmem_limit_bytes=35 * 1024 * 1024),
        cost_estimate=pl.CostEstimate(flops=50_000_000_000, bytes_accessed=100_000_000, transcendentals=0),
        name="factors",
    )(v, matrix, factors)


TILE = 512


def update_kernel(matrix_ref, right_ref, high_ref, low_ref, w_in, out_ref, w_out):
    right = right_ref[...]
    change = contract(high_ref[...], right, 1, 1, None)
    low_v, low_y = low_ref[:, 0 : 2 * LANES], low_ref[:, 2 * LANES :]
    change = change + contract(low_v, right[:, LANES : 3 * LANES], 1, 1, None)
    change = change + contract(low_y, right[:, 4 * LANES :], 1, 1, None)
    out_ref[...] = matrix_ref[...] - change
    w_out[...] = w_in[...]


def update_call(matrix, right, left_high, left_low, w):
    height, length = matrix.shape

    return pl.pallas_call(
        update_kernel,
        grid=(length // TILE,),
        out_shape=(jax.ShapeDtypeStruct(matrix.shape, F32), jax.ShapeDtypeStruct(w.shape, F32)),
        in_specs=[
            pl.BlockSpec((height, TILE), lambda tile: (0, tile)),
            pl.BlockSpec((TILE, right.shape[1]), lambda tile: (tile, 0)),
            *in_vmem(3),
        ],
        out_specs=[pl.BlockSpec((height, TILE), lambda tile: (0, tile)), pl.BlockSpec(w.shape, lambda tile: (0, 0))],
        compiler_params=pltpu.CompilerParams(dimension_semantics=("arbitrary",), vmem_limit_bytes=22 * 1024 * 1024),
        name="update",
    )(matrix, right, left_high, left_low, w)


def per_device(trailing, v_panels, t_panels):
    panels, width, share = v_panels.shape
    size = panels * width
    v = v_panels.reshape(size, share)
    right, left_high, left_low, w = factors_call(v, trailing, t_panels)
    matrix, w = update_call(trailing, right, left_high, left_low, w)
    return (matrix, w.reshape(panels, width, share))


def solution(mesh):
    return jax.shard_map(
        per_device,
        mesh=mesh,
        in_specs=(P("pr", "pc"), P(None, None, ("pr", "pc")), P()),
        out_specs=(P("pr", "pc"), P(None, None, ("pr", "pc"))),
        check_vma=False,
    )
```

```python
import functools

import jax
import jax.numpy as jnp
from jax import lax
from jax.experimental import pallas as pl
from jax.experimental.pallas import tpu as pltpu
from jax.sharding import PartitionSpec as P

HIGHEST = lax.Precision.HIGHEST
MESH = pl.DeviceIdType.MESH
SIDE = 4


class Place:
    def __init__(self):
        pr, pc = lax.axis_index("pr"), lax.axis_index("pc")
        self.x, self.z = lax.rem(pr, SIDE), lax.div(pr, SIDE)
        self.y, self.core = lax.div(pc, 2), lax.rem(pc, 2)

    def at(self, x=0, y=0, z=0, other_core=False):
        far_x = lax.rem(self.x + x + SIDE, SIDE)
        far_y = lax.rem(self.y + y + SIDE, SIDE)
        far_z = lax.rem(self.z + z + SIDE, SIDE)
        core = 1 - self.core if other_core else self.core
        return far_z * SIDE + far_x, far_y * 2 + core

    def spread_to(self):
        block = lax.div(self.x, 2)
        keep = jnp.where(self.core == block, 1, 0)
        far_x = keep * self.x + (1 - keep) * (SIDE - 1 - self.x)
        return lax.rem(self.y + self.z, SIDE) * SIDE + far_x, self.z * 2 + block

    def spread_slot(self):
        block = lax.div(self.x, 2)
        return (self.x - 2 * block) * 8 + 2 * self.y + self.core

    def spread_from(self):
        keep = jnp.where(lax.div(self.x, 2) == self.core, 1, 0)
        far_x = keep * self.x + (1 - keep) * (SIDE - 1 - self.x)
        core = keep * self.core + (1 - keep) * (1 - self.core)
        return self.y * SIDE + far_x, lax.rem(self.z - self.y + SIDE, SIDE) * 2 + core

    def column_slot(self, x=0, z=0):
        far_x = lax.rem(self.x + x + SIDE, SIDE)
        far_z = lax.rem(self.z + z + SIDE, SIDE)
        keep = jnp.where(lax.div(far_x, 2) == self.core, 1, 0)
        from_x = keep * far_x + (1 - keep) * (SIDE - 1 - far_x)
        core = keep * self.core + (1 - keep) * (1 - self.core)
        return (from_x - 2 * self.core) * 8 + 2 * lax.rem(far_z - self.y + SIDE, SIDE) + core

    def row_slot(self, y=0, other_core=False):
        core = 1 - self.core if other_core else self.core
        return lax.rem(self.y + y + SIDE, SIDE) * 2 + core


class Mail:
    def __init__(self, send_sem, recv_sem):
        self.send_sem, self.recv_sem = send_sem, recv_sem
        self.count, self.sent = 0, []

    def number(self):
        self.count += 1
        return self.count - 1

    def copy(self, number, source, target, device):
        return pltpu.make_async_remote_copy(
            src_ref=source,
            dst_ref=target,
            send_sem=self.send_sem.at[number],
            recv_sem=self.recv_sem.at[number],
            device_id=device,
            device_id_type=MESH,
        )

    def send(self, number, source, target, device):
        copy = self.copy(number, source, target, device)
        copy.start()
        self.sent.append(copy)

    def receive(self, number, landed, device):
        self.copy(number, landed, landed, device).wait_recv()

    def finish(self):
        for copy in self.sent:
            copy.wait_send()


def is_here(device, place):
    pr, pc = place.at()
    return jnp.logical_and(device[0] == pr, device[1] == pc)


def spans(rows):
    half = rows // 2
    cut = -(-half // 16) * 8
    first, second = pl.ds(0, half), pl.ds(half, half)
    return (
        first,
        second,
        (pl.ds(0, cut), pl.ds(cut, half - cut)),
        (pl.ds(half, cut), pl.ds(half + cut, half - cut)),
    )


class Spread:
    def __init__(self, place, mail, back=False):
        self.mail, self.number = mail, mail.number()
        self.target = place.spread_from() if back else place.spread_to()
        self.source = place.spread_to() if back else place.spread_from()
        self.stays = is_here(self.target, place)

    def start(self, own, landing, landed, local_sem):
        self.own, self.landed = own, landed
        self.local = pltpu.make_async_copy(own, landed, local_sem)
        self.remote = self.mail.copy(self.number, own, landing, self.target)

        @pl.when(jnp.logical_not(self.stays))
        def _():
            self.remote.start()

        @pl.when(self.stays)
        def _():
            self.local.start()

    def arrived(self):
        @pl.when(jnp.logical_not(self.stays))
        def _():
            self.mail.copy(self.number, self.own, self.landed, self.source).wait_recv()

        @pl.when(self.stays)
        def _():
            self.local.wait()

    def finish(self):
        @pl.when(jnp.logical_not(self.stays))
        def _():
            self.remote.wait_send()


class RowRing:
    def __init__(self, place, mail, own, row, local_sem):
        self.place, self.mail, self.own, self.row = place, mail, own, row
        self.first, self.second, _, _ = spans(own.shape[0])
        self.up, self.down, self.up_on, self.down_on = (mail.number() for _ in range(4))
        self.cross = [mail.number() for _ in range(4)]
        self.partner = place.at(other_core=True)
        self.near_up, self.near_down = place.at(y=1), place.at(y=-1)
        self.keep = pltpu.make_async_copy(own, row.at[place.row_slot()], local_sem)

    def start(self):
        here = self.row.at[self.place.row_slot()]
        self.keep.start()
        self.mail.send(self.up, self.own, here, self.near_up)
        self.mail.send(self.down, self.own, here, self.near_down)
        self.mail.send(self.cross[0], self.own, here, self.partner)

    def near(self):
        mail, row = self.mail, self.row
        below, above = self.place.row_slot(y=-1), self.place.row_slot(y=1)
        mail.receive(self.up, row.at[below], self.near_down)
        mail.send(self.up_on, row.at[below, self.first], row.at[below, self.first], self.near_up)
        mail.send(self.cross[1], row.at[below], row.at[below], self.partner)
        mail.receive(self.down, row.at[above], self.near_up)
        mail.send(self.down_on, row.at[above, self.second], row.at[above, self.second], self.near_down)
        mail.send(self.cross[2], row.at[above], row.at[above], self.partner)

    def far(self):
        mail, row = self.mail, self.row
        far = self.place.row_slot(y=2)
        mail.receive(self.up_on, row.at[far, self.first], self.near_down)
        mail.receive(self.down_on, row.at[far, self.second], self.near_up)
        mail.send(self.cross[3], row.at[far], row.at[far], self.partner)

    def end(self):
        for number, y in ((0, 0), (1, -1), (2, 1), (3, 2)):
            landed = self.row.at[self.place.row_slot(y=y, other_core=True)]
            self.mail.receive(self.cross[number], landed, self.partner)
        self.keep.wait()


OTHER = {"x": "z", "z": "x"}


class ColumnRings:
    def __init__(self, place, mail, col):
        self.place, self.mail, self.col, self.numbers = place, mail, col, {}
        first, second, first_cut, second_cut = spans(col.shape[1])
        self.halves = {"x": (first, first_cut), "z": (second, second_cut)}

    def number(self, *key):
        if key not in self.numbers:
            self.numbers[key] = self.mail.number()
        return self.numbers[key]

    def ref(self, axis, along, across, span):
        x, z = (along, across) if axis == "x" else (across, along)
        return self.col.at[self.place.column_slot(x=x, z=z), span]

    def to(self, axis, step):
        return self.place.at(**{axis: step})

    def push(self, axis, step, half, across, span, along=0):
        ref = self.ref(axis, along, across, span)
        self.mail.send(self.number(axis, step, half, across, along), ref, ref, self.to(axis, step))

    def pull(self, axis, step, half, across, span, along=0):
        ref = self.ref(axis, along - step, across, span)
        self.mail.receive(self.number(axis, step, half, across, along), ref, self.to(axis, -step))

    def pass_on(self, axis, half, across):
        span = self.halves[half][0]
        for step in (1, -1):
            self.push(axis, step, half, across, span)
        if half == axis:
            ref = self.ref(axis, 0, across, span)
            self.mail.send(self.number(axis, "far", half, across), ref, ref, self.to(axis, 2))

    def take(self, axis, step, half, across):
        self.pull(axis, step, half, across, self.halves[half][0])
        if half != axis:
            self.push(axis, step, half, across, self.halves[half][1][0 if step == 1 else 1], along=-step)

    def take_far(self, axis, half, across):
        if half == axis:
            ref = self.ref(axis, 2, across, self.halves[half][0])
            self.mail.receive(self.number(axis, "far", half, across), ref, self.to(axis, 2))
        else:
            for step, part in ((1, 0), (-1, 1)):
                self.pull(axis, step, half, across, self.halves[half][1][part], along=-step)

    def start(self):
        for axis in ("x", "z"):
            self.pass_on(axis, axis, 0)
        for axis in ("x", "z"):
            self.pass_on(axis, OTHER[axis], 0)

    def first_ring(self):
        for step in (1, -1):
            for axis in ("x", "z"):
                self.take(axis, step, axis, 0)
                self.pass_on(OTHER[axis], axis, -step)

    def first_ring_far(self):
        for axis in ("x", "z"):
            self.take_far(axis, axis, 0)
            self.pass_on(OTHER[axis], axis, 2)

    def second_ring(self, across):
        for step in (1, -1):
            for axis in ("x", "z"):
                self.take(axis, step, OTHER[axis], across)

    def last(self):
        for across in (0, -1, 1, 2):
            for axis in ("x", "z"):
                self.take_far(axis, OTHER[axis], across)


def greet(place, far):
    barrier = pltpu.get_barrier_semaphore()
    near = [place.at(x=1), place.at(x=-1), place.at(z=1), place.at(z=-1), place.at(y=1), place.at(y=-1)]
    near.append(place.at(other_core=True))
    if far:
        near += [place.at(x=2), place.at(y=2), place.at(z=2)]
    target, source = place.spread_to(), place.spread_from()
    moves = jnp.logical_not(is_here(target, place))
    for device in near:
        pl.semaphore_signal(barrier, inc=1, device_id=device, device_id_type=MESH)

    @pl.when(moves)
    def _():
        for device in (target, source):
            pl.semaphore_signal(barrier, inc=1, device_id=device, device_id_type=MESH)

    return len(near) + jnp.where(moves, 2, 0)


HIGH = lax.Precision.HIGH
BF16 = jnp.bfloat16
F32 = jnp.float32
LANES = 128
WIDE = 2 * LANES


def contract(left_side, right_side, left_dim, right_dim, precision=HIGHEST):
    return lax.dot_general(
        left_side,
        right_side,
        (((left_dim,), (right_dim,)), ((), ())),
        precision=precision,
        preferred_element_type=F32,
    )


def split(value):
    high = value.astype(BF16).astype(F32)
    return high, value - high


def left_lanes(shape):
    return lax.broadcasted_iota(jnp.int32, shape, len(shape) - 1) < LANES // 2


def swap_halves(value):
    return pltpu.roll(value, LANES // 2, 1)


def unpack(packed, wide, start):
    rows = packed.shape[0] // 3
    tail = packed[pl.ds(2 * rows, rows), :]
    left = left_lanes(tail.shape)
    wide[pl.ds(start, 2 * rows), 0:LANES] = packed[pl.ds(0, 2 * rows), :]
    wide[pl.ds(start, rows), LANES:WIDE] = jnp.where(left, tail, 0.0)
    wide[pl.ds(start + rows, rows), LANES:WIDE] = jnp.where(left, swap_halves(tail), 0.0)


def unpack_split(packed, parts, start, lane=0):
    rows = packed.shape[0] // 3
    high, low = split(packed[pl.ds(0, 2 * rows), :])
    parts[pl.ds(start, 2 * rows), lane : lane + LANES] = low.astype(BF16)
    parts[pl.ds(start, 2 * rows), lane + LANES : lane + 2 * LANES] = high.astype(BF16)
    high, low = split(packed[pl.ds(2 * rows, rows), :])
    left = left_lanes(high.shape)
    ends = slice(lane + 2 * LANES, lane + 3 * LANES)
    parts[pl.ds(start, rows), ends] = jnp.where(left, high, swap_halves(low)).astype(BF16)
    parts[pl.ds(start + rows, rows), ends] = jnp.where(left, swap_halves(high), low).astype(BF16)


def coefficient_steps(panels, width, total_ref, factor_ref, of_y, of_v, of_w):
    size = panels * width

    def begin():
        rows = lax.broadcasted_iota(jnp.int32, (size, WIDE), 0)
        cols = lax.broadcasted_iota(jnp.int32, (size, WIDE), 1)
        eye = jnp.where(rows == cols, 1.0, 0.0)
        zero = jnp.zeros((size, WIDE), F32)
        for ref, first, at in ((of_y, 0, 2), (of_v, 2 * size, 1)):
            ref[:, 0:LANES] = total_ref[pl.ds(first, size), :]
            ref[:, LANES:WIDE] = total_ref[pl.ds(first + size, size), :]
            ref[:, WIDE * at : WIDE * (at + 1)] = eye
            ref[:, WIDE * (3 - at) : WIDE * (4 - at)] = zero

    def step(panel):
        start = panel * width
        here = slice(start, start + width)
        of_x = of_y[here, :]
        if panel:
            before = slice(0, start)
            of_x = of_x - contract(of_w[before, here], of_v[before, :], 0, 0)
            of_x = of_x - contract(of_v[before, here], of_w[before, :], 0, 0)
        factor = factor_ref[here, factor_ref.shape[1] - width :]
        scaled = contract(factor, of_x, 0, 0)
        middle = contract(scaled[:, here], factor, 1, 0)
        of_w[here, :] = scaled - 0.5 * contract(middle, of_v[here, :], 1, 0)

    return begin, step


CHUNK = 128
NEAR = [(x, z) for x in (0, 1, -1) for z in (0, 1, -1)]
FAR = [(x, z) for x in (0, 1, -1, 2) for z in (0, 1, -1, 2) if 2 in (x, z)]


def factors_kernel(
    panels,
    width,
    v_ref,
    matrix,
    right,
    left_high,
    left_low,
    w_ref,
    stage,
    high,
    low,
    row_v,
    row_y,
    col_v,
    col_y,
    row_wide,
    flat_v,
    wide_y,
    partial,
    swap,
    sums,
    near,
    share_sum,
    own,
    v_own,
    grams_ref,
    total_ref,
    grams_swap,
    grams_sum,
    grams_y,
    grams_x,
    grams_z,
    of_y,
    of_v,
    of_w,
    mixing,
    share_v,
    share_y,
    send_sem,
    recv_sem,
    local_sem,
    stage_sem,
):
    place = Place()
    rows = own.shape[0]
    size = panels * width
    share = v_ref.shape[1] - width
    chunks = matrix.shape[0] // CHUNK
    partner = place.at(other_core=True)

    def load(chunk):
        return pltpu.make_async_copy(matrix.at[pl.ds(chunk * CHUNK, CHUNK)], stage.at[chunk % 2], stage_sem.at[chunk % 2])

    v_here = pltpu.make_async_copy(v_ref, v_own, local_sem.at[0])
    v_here.start()
    load(0).start()
    load(1).start()
    greeted = greet(place, True)
    mixing[...] = jnp.zeros_like(mixing)
    v_here.wait()
    mixing[0:size, 0:share] = v_own[:, 0:share]
    turned = mixing[:, 0:WIDE].T
    own[0:share, :] = turned[0:share, 0:LANES]
    near_rows, far_rows = turned[0 : share // 2, LANES:], turned[share // 2 : share, LANES:]
    own[share:, :] = jnp.where(left_lanes(near_rows.shape), near_rows, swap_halves(far_rows))
    pl.semaphore_wait(pltpu.get_barrier_semaphore(), greeted)
    mail = Mail(send_sem, recv_sem)
    spread_v, spread_y = Spread(place, mail), Spread(place, mail)
    ring_v = RowRing(place, mail, own, row_v, local_sem.at[2])
    ring_y = RowRing(place, mail, share_sum, row_y, local_sem.at[4])
    rings_v, rings_y = ColumnRings(place, mail, col_v), ColumnRings(place, mail, col_y)
    mine = place.column_slot()
    todo = list(range(chunks))

    def convert(count):
        for _ in range(count):
            chunk = todo.pop(0)
            load(chunk).wait()
            top, rest = split(stage[chunk % 2])
            high[pl.ds(chunk * CHUNK, CHUNK), :] = top.astype(BF16)
            low[pl.ds(chunk * CHUNK, CHUNK), :] = rest.astype(BF16)
            if chunk + 2 < chunks:
                load(chunk + 2).start()

    def unpack_columns(col, lane, chips):
        for x, z in chips:
            slot = place.column_slot(x=x, z=z)
            unpack_split(col.at[slot], right, pl.multiple_of(slot * share, 32), lane)

    spread_v.start(own, col_v.at[place.spread_slot()], col_v.at[mine], local_sem.at[0])
    convert(4)
    spread_v.arrived()
    rings_v.start()
    ring_v.start()
    convert(2)
    rings_v.first_ring()
    ring_v.near()
    convert(1)
    rings_v.second_ring(0)
    convert(1)
    rings_v.first_ring_far()
    ring_v.far()
    convert(1)
    rings_v.second_ring(-1)
    convert(1)
    rings_v.second_ring(1)
    rings_v.second_ring(2)
    ring_v.end()
    for slot in range(8):
        unpack(row_v.at[slot], row_wide, slot * share)
    flat_v[...] = row_wide[...].T[0:size, :]
    gram = contract(flat_v[...], row_wide[...], 1, 0, HIGH) * 0.125
    grams_ref[2 * size : 3 * size, :] = gram[:, 0:LANES]
    grams_ref[3 * size : 4 * size, :] = gram[:, LANES:]
    unpack_columns(col_v, 0, NEAR)
    rings_v.last()
    unpack_columns(col_v, 0, FAR)

    first, second, _, _ = spans(rows)
    near_up, near_down = place.at(y=1), place.at(y=-1)
    across = {y: mail.number() for y in (2, 1, -1, 0)}
    far_up, far_down, up_now, up_later, down_now, down_later = (mail.number() for _ in range(6))
    left = left_lanes((share // 2, LANES))

    def product(y):
        block = lax.rem(place.y + y + SIDE, SIDE)
        here = pl.ds(pl.multiple_of(block * 2 * share, 2 * share), 2 * share)
        top = jnp.dot(high[here, :], right[:, 0 : 3 * LANES], preferred_element_type=F32)
        rest = jnp.dot(low[here, :], right[:, LANES : 3 * LANES], preferred_element_type=F32)
        main = top[:, 0:LANES] + top[:, LANES : 2 * LANES] + rest[:, 0:LANES]
        tail = top[:, 2 * LANES :] + rest[:, LANES:]
        tail = tail + swap_halves(tail)
        wide_y[here, 0:LANES] = main
        wide_y[here, LANES:WIDE] = jnp.where(left_lanes(tail.shape), tail, 0.0)
        for core in range(2):
            slot = (y % SIDE) * 2 + core
            start = core * share
            partial[slot, 0:share, :] = main[start : start + share]
            upper, lower = tail[start : start + share // 2], tail[start + share // 2 : start + share]
            partial[slot, share:, :] = jnp.where(left, upper, lower)
        slot = (y % SIDE) * 2 + 1 - place.core
        mail.send(across[y], partial.at[slot], swap.at[y % SIDE], partner)

    def add_across(y):
        slot = y % SIDE
        mail.receive(across[y], swap.at[slot], partner)
        sums[slot, :, :] = partial[slot * 2 + place.core] + swap[slot]

    product(2)
    product(1)
    add_across(2)
    mail.send(far_up, sums.at[2, first], near.at[0, first], near_up)
    mail.send(far_down, sums.at[2, second], near.at[0, second], near_down)
    product(-1)
    add_across(1)
    mail.send(up_now, sums.at[1, second], near.at[1, second], near_up)
    product(0)
    add_across(-1)
    mail.send(down_now, sums.at[3, first], near.at[2, first], near_down)
    gram = contract(flat_v[...], wide_y[...], 1, 0, HIGH)
    grams_ref[0:size, :] = gram[:, 0:LANES]
    grams_ref[size : 2 * size, :] = gram[:, LANES:]

    half = grams_ref.shape[0] // 2
    part = half // SIDE
    cores = mail.number()
    mail.send(cores, grams_ref.at[pl.ds(pl.multiple_of((1 - place.core) * half, 8), half)], grams_swap, partner)

    def exchange(axis, source, landing):
        numbers = [mail.number() for _ in range(1, SIDE)]
        for step in range(1, SIDE):
            mail.send(numbers[step - 1], source(step), landing.at[step - 1], place.at(**{axis: step}))

        def arrived():
            for step in range(1, SIDE):
                mail.receive(numbers[step - 1], landing.at[step - 1], place.at(**{axis: -step}))
            return landing[0] + landing[1] + landing[2]

        return arrived

    def quarter(step):
        return pl.ds(pl.multiple_of(lax.rem(place.y + step, SIDE) * part, 8), part)

    mail.receive(far_up, near.at[0, first], near_down)
    sums[1, first, :] = sums[1, first, :] + near[0, first, :]
    mail.send(up_later, sums.at[1, first], near.at[1, first], near_up)
    mail.receive(far_down, near.at[0, second], near_up)
    sums[3, second, :] = sums[3, second, :] + near[0, second, :]
    mail.send(down_later, sums.at[3, second], near.at[2, second], near_down)
    add_across(0)
    mail.receive(cores, grams_swap, partner)
    core_half = pl.ds(pl.multiple_of(place.core * half, 8), half)
    grams_sum[pl.ds(0, half), :] = grams_ref[core_half, :] + grams_swap[...]
    over_y = exchange("y", lambda step: grams_sum.at[quarter(step)], grams_y)
    mail.receive(up_now, near.at[1, second], near_down)
    mail.receive(down_now, near.at[2, first], near_up)
    mail.receive(up_later, near.at[1, first], near_down)
    mail.receive(down_later, near.at[2, second], near_up)
    share_sum[...] = sums[0] + near[1] + near[2]

    spread_y.start(share_sum, col_y.at[place.spread_slot()], col_y.at[mine], local_sem.at[1])
    grams_sum[pl.ds(half, part), :] = grams_sum[quarter(0), :] + over_y()
    over_x = exchange("x", lambda step: grams_sum.at[pl.ds(half, part)], grams_x)
    spread_y.arrived()
    rings_y.start()
    ring_y.start()
    grams_sum[pl.ds(half + part, part), :] = grams_sum[pl.ds(half, part), :] + over_x()
    over_z = exchange("z", lambda step: grams_sum.at[pl.ds(half + part, part)], grams_z)

    def total_rows(y, other_core=False):
        core = 1 - place.core if other_core else place.core
        start = core * half + lax.rem(place.y + y + SIDE, SIDE) * part
        return total_ref.at[pl.ds(pl.multiple_of(start, 8), part)]

    back_y = [mail.number() for _ in range(1, SIDE)]
    back_core = [mail.number() for _ in range(SIDE)]
    rings_y.first_ring()
    ring_y.near()
    start = place.core * half + place.y * part
    total_ref[pl.ds(pl.multiple_of(start, 8), part), :] = grams_sum[pl.ds(half + part, part), :] + over_z()
    for step in range(1, SIDE):
        mail.send(back_y[step - 1], total_rows(0), total_rows(0), place.at(y=step))
    mail.send(back_core[0], total_rows(0), total_rows(0), partner)
    rings_y.second_ring(0)
    rings_y.first_ring_far()
    ring_y.far()
    rings_y.second_ring(-1)
    for step in range(1, SIDE):
        mail.receive(back_y[step - 1], total_rows(-step), place.at(y=-step))
        mail.send(back_core[step], total_rows(-step), total_rows(-step), partner)
    rings_y.second_ring(1)
    for step in range(SIDE):
        mail.receive(back_core[step], total_rows(-step, True), partner)

    begin, step = coefficient_steps(panels, width, total_ref, v_own, of_y, of_v, of_w)

    def mix():
        mixing[...] = jnp.zeros_like(mixing)
        of_d, of_c = of_w[:, WIDE : 2 * WIDE], of_w[:, 2 * WIDE :]
        mixing[0:size, 0:WIDE] = of_d
        mixing[:, 0:WIDE] = mixing[:, 0:WIDE] + mixing[:, 0:WIDE].T
        mixing[0:size, WIDE:] = of_c

    def store_left(value, start, lane, low_lane):
        left = left_lanes((share, LANES))
        for at in range(2):
            top, rest = split(value[:, at * LANES : (at + 1) * LANES])
            if at:
                top = jnp.where(left, top, swap_halves(top))
                rest = jnp.where(left, rest, swap_halves(rest))
            here = pl.ds(start, share)
            low_here = slice(low_lane + at * LANES, low_lane + (at + 1) * LANES)
            left_low[here, low_here] = rest.astype(BF16)
            if not at:
                left_high[here, lane : lane + LANES] = top.astype(BF16)
            left_high[here, lane + (at + 1) * LANES : lane + (at + 2) * LANES] = top.astype(BF16)

    def left_rows(slot):
        unpack(row_y.at[slot], share_y, 0)
        here = pl.ds(slot * share, share)
        of_right_v = contract(row_wide[here, :], mixing[:, 0:WIDE], 1, 0, HIGH)
        of_right_v = of_right_v + contract(share_y[...], mixing[:, WIDE:], 1, 1, HIGH)
        of_right_y = contract(row_wide[here, :], mixing[:, WIDE:], 1, 0, HIGH)
        store_left(of_right_v, slot * share, 0, 0)
        store_left(of_right_y, slot * share, 3 * LANES, 2 * LANES)

    begin()
    step(0)
    rings_y.second_ring(2)
    step(1)
    step(2)
    step(3)
    step(4)
    step(5)
    mix()
    unpack(own, share_v, 0)
    unpack(share_sum, share_y, 0)
    w_ref[...] = contract(of_w[:, WIDE : 2 * WIDE], share_v[...], 1, 1, HIGH)
    w_ref[...] = w_ref[...] + contract(of_w[:, 2 * WIDE :], share_y[...], 1, 1, HIGH)
    ring_y.end()
    for slot in range(8):
        left_rows(slot)
    unpack_columns(col_y, 3 * LANES, NEAR)
    rings_y.last()
    unpack_columns(col_y, 3 * LANES, FAR)
    spread_v.finish()
    spread_y.finish()
    mail.finish()


def in_vmem(count):
    return [pl.BlockSpec(memory_space=pltpu.VMEM)] * count


def factors_call(v, matrix, panels, width):
    size, share = v.shape[0], v.shape[1] - width
    rows, lanes = share + share // 2, LANES
    height, length = matrix.shape
    grams = 4 * size
    part = grams // 8
    return pl.pallas_call(
        functools.partial(factors_kernel, panels, width),
        out_shape=(
            jax.ShapeDtypeStruct((length, 6 * lanes), BF16),
            jax.ShapeDtypeStruct((height, 6 * lanes), BF16),
            jax.ShapeDtypeStruct((height, 4 * lanes), BF16),
            jax.ShapeDtypeStruct((size, share), F32),
        ),
        in_specs=[pl.BlockSpec(memory_space=pltpu.HBM)] * 2,
        out_specs=in_vmem(4),
        scratch_shapes=[
            pltpu.VMEM((2, CHUNK, length), F32),
            pltpu.VMEM((height, length), BF16),
            pltpu.VMEM((height, length), BF16),
            pltpu.VMEM((8, rows, lanes), F32),
            pltpu.VMEM((8, rows, lanes), F32),
            pltpu.VMEM((16, rows, lanes), F32),
            pltpu.VMEM((16, rows, lanes), F32),
            pltpu.VMEM((height, WIDE), F32),
            pltpu.VMEM((size, height), F32),
            pltpu.VMEM((height, WIDE), F32),
            pltpu.VMEM((8, rows, lanes), F32),
            pltpu.VMEM((SIDE, rows, lanes), F32),
            pltpu.VMEM((SIDE, rows, lanes), F32),
            pltpu.VMEM((3, rows, lanes), F32),
            pltpu.VMEM((rows, lanes), F32),
            pltpu.VMEM((rows, lanes), F32),
            pltpu.VMEM(v.shape, F32),
            pltpu.VMEM((grams, lanes), F32),
            pltpu.VMEM((grams, lanes), F32),
            pltpu.VMEM((SIDE * part, lanes), F32),
            pltpu.VMEM((6 * part, lanes), F32),
            pltpu.VMEM((3, part, lanes), F32),
            pltpu.VMEM((3, part, lanes), F32),
            pltpu.VMEM((3, part, lanes), F32),
            pltpu.VMEM((size, 3 * WIDE), F32),
            pltpu.VMEM((size, 3 * WIDE), F32),
            pltpu.VMEM((size, 3 * WIDE), F32),
            pltpu.VMEM((WIDE, 2 * WIDE), F32),
            pltpu.VMEM((share, WIDE), F32),
            pltpu.VMEM((share, WIDE), F32),
            pltpu.SemaphoreType.DMA((192,)),
            pltpu.SemaphoreType.DMA((192,)),
            pltpu.SemaphoreType.DMA((5,)),
            pltpu.SemaphoreType.DMA((2,)),
        ],
        compiler_params=pltpu.CompilerParams(collective_id=0, has_side_effects=True, vmem_limit_bytes=35 * 1024 * 1024),
        cost_estimate=pl.CostEstimate(flops=50_000_000_000, bytes_accessed=100_000_000, transcendentals=0),
        name="factors",
    )(v, matrix)


TILE = 512


def update_kernel(matrix_ref, right_ref, high_ref, low_ref, w_in, out_ref, w_out):
    right = right_ref[...]
    change = contract(high_ref[...], right, 1, 1, None)
    low_v, low_y = low_ref[:, 0 : 2 * LANES], low_ref[:, 2 * LANES :]
    change = change + contract(low_v, right[:, LANES : 3 * LANES], 1, 1, None)
    change = change + contract(low_y, right[:, 4 * LANES :], 1, 1, None)
    out_ref[...] = matrix_ref[...] - change
    w_out[...] = w_in[...]


def update_call(matrix, right, left_high, left_low, w):
    height, length = matrix.shape

    return pl.pallas_call(
        update_kernel,
        grid=(length // TILE,),
        out_shape=(jax.ShapeDtypeStruct(matrix.shape, F32), jax.ShapeDtypeStruct(w.shape, F32)),
        in_specs=[
            pl.BlockSpec((height, TILE), lambda tile: (0, tile)),
            pl.BlockSpec((TILE, right.shape[1]), lambda tile: (tile, 0)),
            *in_vmem(3),
        ],
        out_specs=[pl.BlockSpec((height, TILE), lambda tile: (0, tile)), pl.BlockSpec(w.shape, lambda tile: (0, 0))],
        compiler_params=pltpu.CompilerParams(dimension_semantics=("arbitrary",), vmem_limit_bytes=22 * 1024 * 1024),
        name="update",
    )(matrix, right, left_high, left_low, w)


def per_device(trailing, v_panels, t_panels):
    panels, width, share = v_panels.shape
    size = panels * width
    v = jnp.concatenate([v_panels, t_panels], axis=2).reshape(size, share + width)
    right, left_high, left_low, w = factors_call(v, trailing, panels, width)
    matrix, w = update_call(trailing, right, left_high, left_low, w)
    return (matrix, w.reshape(panels, width, share))


def solution(mesh):
    return jax.shard_map(
        per_device,
        mesh=mesh,
        in_specs=(P("pr", "pc"), P(None, None, ("pr", "pc")), P()),
        out_specs=(P("pr", "pc"), P(None, None, ("pr", "pc"))),
        check_vma=False,
    )
```

```python
import functools

import jax
import jax.numpy as jnp
from jax import lax
from jax.experimental import pallas as pl
from jax.experimental.pallas import tpu as pltpu
from jax.sharding import PartitionSpec as P

HIGHEST = lax.Precision.HIGHEST
MESH = pl.DeviceIdType.MESH
SIDE = 4


class Place:
    def __init__(self):
        pr, pc = lax.axis_index("pr"), lax.axis_index("pc")
        self.x, self.z = lax.rem(pr, SIDE), lax.div(pr, SIDE)
        self.y, self.core = lax.div(pc, 2), lax.rem(pc, 2)

    def at(self, x=0, y=0, z=0, other_core=False):
        far_x = lax.rem(self.x + x + SIDE, SIDE)
        far_y = lax.rem(self.y + y + SIDE, SIDE)
        far_z = lax.rem(self.z + z + SIDE, SIDE)
        core = 1 - self.core if other_core else self.core
        return far_z * SIDE + far_x, far_y * 2 + core

    def spread_to(self):
        block = lax.div(self.x, 2)
        keep = jnp.where(self.core == block, 1, 0)
        far_x = keep * self.x + (1 - keep) * (SIDE - 1 - self.x)
        return lax.rem(self.y + self.z, SIDE) * SIDE + far_x, self.z * 2 + block

    def spread_slot(self):
        block = lax.div(self.x, 2)
        return (self.x - 2 * block) * 8 + 2 * self.y + self.core

    def spread_from(self):
        keep = jnp.where(lax.div(self.x, 2) == self.core, 1, 0)
        far_x = keep * self.x + (1 - keep) * (SIDE - 1 - self.x)
        core = keep * self.core + (1 - keep) * (1 - self.core)
        return self.y * SIDE + far_x, lax.rem(self.z - self.y + SIDE, SIDE) * 2 + core

    def column_slot(self, x=0, z=0):
        far_x = lax.rem(self.x + x + SIDE, SIDE)
        far_z = lax.rem(self.z + z + SIDE, SIDE)
        keep = jnp.where(lax.div(far_x, 2) == self.core, 1, 0)
        from_x = keep * far_x + (1 - keep) * (SIDE - 1 - far_x)
        core = keep * self.core + (1 - keep) * (1 - self.core)
        return (from_x - 2 * self.core) * 8 + 2 * lax.rem(far_z - self.y + SIDE, SIDE) + core

    def row_slot(self, y=0, other_core=False):
        core = 1 - self.core if other_core else self.core
        return lax.rem(self.y + y + SIDE, SIDE) * 2 + core


class Mail:
    def __init__(self, send_sem, recv_sem):
        self.send_sem, self.recv_sem = send_sem, recv_sem
        self.count, self.sent = 0, []

    def number(self):
        self.count += 1
        return self.count - 1

    def copy(self, number, source, target, device):
        return pltpu.make_async_remote_copy(
            src_ref=source,
            dst_ref=target,
            send_sem=self.send_sem.at[number],
            recv_sem=self.recv_sem.at[number],
            device_id=device,
            device_id_type=MESH,
        )

    def send(self, number, source, target, device):
        copy = self.copy(number, source, target, device)
        copy.start()
        self.sent.append(copy)

    def receive(self, number, landed, device):
        self.copy(number, landed, landed, device).wait_recv()

    def finish(self):
        for copy in self.sent:
            copy.wait_send()


def is_here(device, place):
    pr, pc = place.at()
    return jnp.logical_and(device[0] == pr, device[1] == pc)


def spans(rows):
    half = rows // 2
    cut = -(-half // 16) * 8
    first, second = pl.ds(0, half), pl.ds(half, half)
    return (
        first,
        second,
        (pl.ds(0, cut), pl.ds(cut, half - cut)),
        (pl.ds(half, cut), pl.ds(half + cut, half - cut)),
    )


class Spread:
    def __init__(self, place, mail, back=False):
        self.mail, self.number = mail, mail.number()
        self.target = place.spread_from() if back else place.spread_to()
        self.source = place.spread_to() if back else place.spread_from()
        self.stays = is_here(self.target, place)

    def start(self, own, landing, landed, local_sem):
        self.own, self.landed = own, landed
        self.local = pltpu.make_async_copy(own, landed, local_sem)
        self.remote = self.mail.copy(self.number, own, landing, self.target)

        @pl.when(jnp.logical_not(self.stays))
        def _():
            self.remote.start()

        @pl.when(self.stays)
        def _():
            self.local.start()

    def arrived(self):
        @pl.when(jnp.logical_not(self.stays))
        def _():
            self.mail.copy(self.number, self.own, self.landed, self.source).wait_recv()

        @pl.when(self.stays)
        def _():
            self.local.wait()

    def finish(self):
        @pl.when(jnp.logical_not(self.stays))
        def _():
            self.remote.wait_send()


class RowRing:
    def __init__(self, place, mail, own, row, local_sem):
        self.place, self.mail, self.own, self.row = place, mail, own, row
        self.first, self.second, _, _ = spans(own.shape[0])
        self.up, self.down, self.up_on, self.down_on = (mail.number() for _ in range(4))
        self.cross = [mail.number() for _ in range(4)]
        self.partner = place.at(other_core=True)
        self.near_up, self.near_down = place.at(y=1), place.at(y=-1)
        self.keep = pltpu.make_async_copy(own, row.at[place.row_slot()], local_sem)

    def start(self):
        here = self.row.at[self.place.row_slot()]
        self.keep.start()
        self.mail.send(self.up, self.own, here, self.near_up)
        self.mail.send(self.down, self.own, here, self.near_down)
        self.mail.send(self.cross[0], self.own, here, self.partner)

    def near(self):
        mail, row = self.mail, self.row
        below, above = self.place.row_slot(y=-1), self.place.row_slot(y=1)
        mail.receive(self.up, row.at[below], self.near_down)
        mail.send(self.up_on, row.at[below, self.first], row.at[below, self.first], self.near_up)
        mail.send(self.cross[1], row.at[below], row.at[below], self.partner)
        mail.receive(self.down, row.at[above], self.near_up)
        mail.send(self.down_on, row.at[above, self.second], row.at[above, self.second], self.near_down)
        mail.send(self.cross[2], row.at[above], row.at[above], self.partner)

    def far(self):
        mail, row = self.mail, self.row
        far = self.place.row_slot(y=2)
        mail.receive(self.up_on, row.at[far, self.first], self.near_down)
        mail.receive(self.down_on, row.at[far, self.second], self.near_up)
        mail.send(self.cross[3], row.at[far], row.at[far], self.partner)

    def end(self):
        for number, y in ((0, 0), (1, -1), (2, 1), (3, 2)):
            landed = self.row.at[self.place.row_slot(y=y, other_core=True)]
            self.mail.receive(self.cross[number], landed, self.partner)
        self.keep.wait()


OTHER = {"x": "z", "z": "x"}


class ColumnRings:
    def __init__(self, place, mail, col):
        self.place, self.mail, self.col, self.numbers = place, mail, col, {}
        first, second, first_cut, second_cut = spans(col.shape[1])
        self.halves = {"x": (first, first_cut), "z": (second, second_cut)}

    def number(self, *key):
        if key not in self.numbers:
            self.numbers[key] = self.mail.number()
        return self.numbers[key]

    def ref(self, axis, along, across, span):
        x, z = (along, across) if axis == "x" else (across, along)
        return self.col.at[self.place.column_slot(x=x, z=z), span]

    def to(self, axis, step):
        return self.place.at(**{axis: step})

    def push(self, axis, step, half, across, span, along=0):
        ref = self.ref(axis, along, across, span)
        self.mail.send(self.number(axis, step, half, across, along), ref, ref, self.to(axis, step))

    def pull(self, axis, step, half, across, span, along=0):
        ref = self.ref(axis, along - step, across, span)
        self.mail.receive(self.number(axis, step, half, across, along), ref, self.to(axis, -step))

    def pass_on(self, axis, half, across):
        span = self.halves[half][0]
        for step in (1, -1):
            self.push(axis, step, half, across, span)
        if half == axis:
            ref = self.ref(axis, 0, across, span)
            self.mail.send(self.number(axis, "far", half, across), ref, ref, self.to(axis, 2))

    def take(self, axis, step, half, across):
        self.pull(axis, step, half, across, self.halves[half][0])
        if half != axis:
            self.push(axis, step, half, across, self.halves[half][1][0 if step == 1 else 1], along=-step)

    def take_far(self, axis, half, across):
        if half == axis:
            ref = self.ref(axis, 2, across, self.halves[half][0])
            self.mail.receive(self.number(axis, "far", half, across), ref, self.to(axis, 2))
        else:
            for step, part in ((1, 0), (-1, 1)):
                self.pull(axis, step, half, across, self.halves[half][1][part], along=-step)

    def start(self):
        for axis in ("x", "z"):
            self.pass_on(axis, axis, 0)
        for axis in ("x", "z"):
            self.pass_on(axis, OTHER[axis], 0)

    def first_ring(self):
        for step in (1, -1):
            for axis in ("x", "z"):
                self.take(axis, step, axis, 0)
                self.pass_on(OTHER[axis], axis, -step)

    def first_ring_far(self):
        for axis in ("x", "z"):
            self.take_far(axis, axis, 0)
            self.pass_on(OTHER[axis], axis, 2)

    def second_ring(self, across):
        for step in (1, -1):
            for axis in ("x", "z"):
                self.take(axis, step, OTHER[axis], across)

    def last(self):
        for across in (0, -1, 1, 2):
            for axis in ("x", "z"):
                self.take_far(axis, OTHER[axis], across)


def greet(place, far):
    barrier = pltpu.get_barrier_semaphore()
    near = [place.at(x=1), place.at(x=-1), place.at(z=1), place.at(z=-1), place.at(y=1), place.at(y=-1)]
    near.append(place.at(other_core=True))
    if far:
        near += [place.at(x=2), place.at(y=2), place.at(z=2)]
    target, source = place.spread_to(), place.spread_from()
    moves = jnp.logical_not(is_here(target, place))
    for device in near:
        pl.semaphore_signal(barrier, inc=1, device_id=device, device_id_type=MESH)

    @pl.when(moves)
    def _():
        for device in (target, source):
            pl.semaphore_signal(barrier, inc=1, device_id=device, device_id_type=MESH)

    return len(near) + jnp.where(moves, 2, 0)


HIGH = lax.Precision.HIGH
BF16 = jnp.bfloat16
F32 = jnp.float32
LANES = 128
WIDE = 2 * LANES


def contract(left_side, right_side, left_dim, right_dim, precision=HIGHEST):
    return lax.dot_general(
        left_side,
        right_side,
        (((left_dim,), (right_dim,)), ((), ())),
        precision=precision,
        preferred_element_type=F32,
    )


def split(value):
    high = value.astype(BF16).astype(F32)
    return high, value - high


def left_lanes(shape):
    return lax.broadcasted_iota(jnp.int32, shape, len(shape) - 1) < LANES // 2


def swap_halves(value):
    return pltpu.roll(value, LANES // 2, 1)


def unpack(packed, wide, start):
    rows = packed.shape[0] // 3
    tail = packed[pl.ds(2 * rows, rows), :]
    left = left_lanes(tail.shape)
    wide[pl.ds(start, 2 * rows), 0:LANES] = packed[pl.ds(0, 2 * rows), :]
    wide[pl.ds(start, rows), LANES:WIDE] = jnp.where(left, tail, 0.0)
    wide[pl.ds(start + rows, rows), LANES:WIDE] = jnp.where(left, swap_halves(tail), 0.0)


def unpack_split(packed, parts, start, lane=0):
    rows = packed.shape[0] // 3
    high, low = split(packed[pl.ds(0, 2 * rows), :])
    parts[pl.ds(start, 2 * rows), lane : lane + LANES] = low.astype(BF16)
    parts[pl.ds(start, 2 * rows), lane + LANES : lane + 2 * LANES] = high.astype(BF16)
    high, low = split(packed[pl.ds(2 * rows, rows), :])
    left = left_lanes(high.shape)
    ends = slice(lane + 2 * LANES, lane + 3 * LANES)
    parts[pl.ds(start, rows), ends] = jnp.where(left, high, swap_halves(low)).astype(BF16)
    parts[pl.ds(start + rows, rows), ends] = jnp.where(left, swap_halves(high), low).astype(BF16)


def coefficient_steps(panels, width, total_ref, factor_ref, of_y, of_v, of_w):
    size = panels * width

    def begin():
        rows = lax.broadcasted_iota(jnp.int32, (size, WIDE), 0)
        cols = lax.broadcasted_iota(jnp.int32, (size, WIDE), 1)
        eye = jnp.where(rows == cols, 1.0, 0.0)
        zero = jnp.zeros((size, WIDE), F32)
        for ref, first, at in ((of_y, 0, 2), (of_v, 2 * size, 1)):
            ref[:, 0:LANES] = total_ref[pl.ds(first, size), :]
            ref[:, LANES:WIDE] = total_ref[pl.ds(first + size, size), :]
            ref[:, WIDE * at : WIDE * (at + 1)] = eye
            ref[:, WIDE * (3 - at) : WIDE * (4 - at)] = zero

    def step(panel):
        start = panel * width
        here = slice(start, start + width)
        of_x = of_y[here, :]
        if panel:
            before = slice(0, start)
            of_x = of_x - contract(of_w[before, here], of_v[before, :], 0, 0)
            of_x = of_x - contract(of_v[before, here], of_w[before, :], 0, 0)
        factor = factor_ref[here, factor_ref.shape[1] - width :]
        scaled = contract(factor, of_x, 0, 0)
        middle = contract(scaled[:, here], factor, 1, 0)
        of_w[here, :] = scaled - 0.5 * contract(middle, of_v[here, :], 1, 0)

    return begin, step


CHUNK = 128
NEAR = [(x, z) for x in (0, 1, -1) for z in (0, 1, -1)]
FAR = [(x, z) for x in (0, 1, -1, 2) for z in (0, 1, -1, 2) if 2 in (x, z)]


def factors_kernel(
    panels,
    width,
    v_ref,
    matrix,
    right,
    left_high,
    left_low,
    w_ref,
    stage,
    high,
    low,
    row_v,
    row_y,
    col_v,
    col_y,
    row_wide,
    flat_v,
    wide_y,
    partial,
    swap,
    sums,
    near,
    share_sum,
    own,
    v_own,
    grams_ref,
    total_ref,
    grams_swap,
    grams_sum,
    grams_y,
    grams_x,
    grams_z,
    of_y,
    of_v,
    of_w,
    mixing,
    share_v,
    share_y,
    send_sem,
    recv_sem,
    local_sem,
    stage_sem,
):
    place = Place()
    rows = own.shape[0]
    size = panels * width
    share = v_ref.shape[1] - width
    chunks = matrix.shape[0] // CHUNK
    partner = place.at(other_core=True)

    def load(chunk):
        return pltpu.make_async_copy(matrix.at[pl.ds(chunk * CHUNK, CHUNK)], stage.at[chunk % 2], stage_sem.at[chunk % 2])

    v_here = pltpu.make_async_copy(v_ref, v_own, local_sem.at[0])
    v_here.start()
    load(0).start()
    load(1).start()
    greeted = greet(place, True)
    mixing[...] = jnp.zeros_like(mixing)
    v_here.wait()
    mixing[0:size, 0:share] = v_own[:, 0:share]
    turned = mixing[:, 0:WIDE].T
    own[0:share, :] = turned[0:share, 0:LANES]
    near_rows, far_rows = turned[0 : share // 2, LANES:], turned[share // 2 : share, LANES:]
    own[share:, :] = jnp.where(left_lanes(near_rows.shape), near_rows, swap_halves(far_rows))
    pl.semaphore_wait(pltpu.get_barrier_semaphore(), greeted)
    mail = Mail(send_sem, recv_sem)
    spread_v, spread_y = Spread(place, mail), Spread(place, mail)
    ring_v = RowRing(place, mail, own, row_v, local_sem.at[2])
    ring_y = RowRing(place, mail, share_sum, row_y, local_sem.at[4])
    rings_v, rings_y = ColumnRings(place, mail, col_v), ColumnRings(place, mail, col_y)
    mine = place.column_slot()
    todo = list(range(chunks))

    def convert(count):
        for _ in range(count):
            chunk = todo.pop(0)
            load(chunk).wait()
            top, rest = split(stage[chunk % 2])
            high[pl.ds(chunk * CHUNK, CHUNK), :] = top.astype(BF16)
            low[pl.ds(chunk * CHUNK, CHUNK), :] = rest.astype(BF16)
            if chunk + 2 < chunks:
                load(chunk + 2).start()

    def unpack_columns(col, lane, chips):
        for x, z in chips:
            slot = place.column_slot(x=x, z=z)
            unpack_split(col.at[slot], right, pl.multiple_of(slot * share, 32), lane)

    spread_v.start(own, col_v.at[place.spread_slot()], col_v.at[mine], local_sem.at[0])
    convert(4)
    spread_v.arrived()
    rings_v.start()
    ring_v.start()
    convert(2)
    rings_v.first_ring()
    ring_v.near()
    convert(1)
    rings_v.second_ring(0)
    convert(1)
    rings_v.first_ring_far()
    ring_v.far()
    convert(1)
    rings_v.second_ring(-1)
    convert(1)
    rings_v.second_ring(1)
    rings_v.second_ring(2)
    ring_v.end()
    for slot in range(8):
        unpack(row_v.at[slot], row_wide, slot * share)
    flat_v[...] = row_wide[...].T[0:size, :]
    gram = contract(flat_v[...], row_wide[...], 1, 0, HIGH) * 0.125
    grams_ref[2 * size : 3 * size, :] = gram[:, 0:LANES]
    grams_ref[3 * size : 4 * size, :] = gram[:, LANES:]
    unpack_columns(col_v, 0, NEAR)
    rings_v.last()
    unpack_columns(col_v, 0, FAR)

    first, second, _, _ = spans(rows)
    near_up, near_down = place.at(y=1), place.at(y=-1)
    across = {y: mail.number() for y in (2, 1, -1, 0)}
    far_up, far_down, up_now, up_later, down_now, down_later = (mail.number() for _ in range(6))
    left = left_lanes((share // 2, LANES))

    def product(y):
        block = lax.rem(place.y + y + SIDE, SIDE)
        here = pl.ds(pl.multiple_of(block * 2 * share, 2 * share), 2 * share)
        top = jnp.dot(high[here, :], right[:, 0 : 3 * LANES], preferred_element_type=F32)
        rest = jnp.dot(low[here, :], right[:, LANES : 3 * LANES], preferred_element_type=F32)
        main = top[:, 0:LANES] + top[:, LANES : 2 * LANES] + rest[:, 0:LANES]
        tail = top[:, 2 * LANES :] + rest[:, LANES:]
        tail = tail + swap_halves(tail)
        wide_y[here, 0:LANES] = main
        wide_y[here, LANES:WIDE] = jnp.where(left_lanes(tail.shape), tail, 0.0)
        for core in range(2):
            slot = (y % SIDE) * 2 + core
            start = core * share
            partial[slot, 0:share, :] = main[start : start + share]
            upper, lower = tail[start : start + share // 2], tail[start + share // 2 : start + share]
            partial[slot, share:, :] = jnp.where(left, upper, lower)
        slot = (y % SIDE) * 2 + 1 - place.core
        mail.send(across[y], partial.at[slot], swap.at[y % SIDE], partner)

    def add_across(y):
        slot = y % SIDE
        mail.receive(across[y], swap.at[slot], partner)
        sums[slot, :, :] = partial[slot * 2 + place.core] + swap[slot]

    product(2)
    product(1)
    add_across(2)
    mail.send(far_up, sums.at[2, first], near.at[0, first], near_up)
    mail.send(far_down, sums.at[2, second], near.at[0, second], near_down)
    product(-1)
    add_across(1)
    mail.send(up_now, sums.at[1, second], near.at[1, second], near_up)
    product(0)
    add_across(-1)
    mail.send(down_now, sums.at[3, first], near.at[2, first], near_down)
    gram = contract(flat_v[...], wide_y[...], 1, 0, HIGH)
    grams_ref[0:size, :] = gram[:, 0:LANES]
    grams_ref[size : 2 * size, :] = gram[:, LANES:]

    half = grams_ref.shape[0] // 2
    part = half // SIDE
    cores = mail.number()
    mail.send(cores, grams_ref.at[pl.ds(pl.multiple_of((1 - place.core) * half, 8), half)], grams_swap, partner)

    def exchange(axis, source, landing):
        numbers = [mail.number() for _ in range(1, SIDE)]
        for step in range(1, SIDE):
            mail.send(numbers[step - 1], source(step), landing.at[step - 1], place.at(**{axis: step}))

        def arrived():
            for step in range(1, SIDE):
                mail.receive(numbers[step - 1], landing.at[step - 1], place.at(**{axis: -step}))
            return landing[0] + landing[1] + landing[2]

        return arrived

    def quarter(step):
        return pl.ds(pl.multiple_of(lax.rem(place.y + step, SIDE) * part, 8), part)

    mail.receive(far_up, near.at[0, first], near_down)
    sums[1, first, :] = sums[1, first, :] + near[0, first, :]
    mail.send(up_later, sums.at[1, first], near.at[1, first], near_up)
    mail.receive(far_down, near.at[0, second], near_up)
    sums[3, second, :] = sums[3, second, :] + near[0, second, :]
    mail.send(down_later, sums.at[3, second], near.at[2, second], near_down)
    add_across(0)
    mail.receive(cores, grams_swap, partner)
    core_half = pl.ds(pl.multiple_of(place.core * half, 8), half)
    grams_sum[pl.ds(0, half), :] = grams_ref[core_half, :] + grams_swap[...]
    over_y = exchange("y", lambda step: grams_sum.at[quarter(step)], grams_y)
    mail.receive(up_now, near.at[1, second], near_down)
    mail.receive(down_now, near.at[2, first], near_up)
    mail.receive(up_later, near.at[1, first], near_down)
    mail.receive(down_later, near.at[2, second], near_up)
    share_sum[...] = sums[0] + near[1] + near[2]

    spread_y.start(share_sum, col_y.at[place.spread_slot()], col_y.at[mine], local_sem.at[1])
    grams_sum[pl.ds(half, part), :] = grams_sum[quarter(0), :] + over_y()
    over_x = exchange("x", lambda step: grams_sum.at[pl.ds(half, part)], grams_x)
    spread_y.arrived()
    rings_y.start()
    ring_y.start()
    grams_sum[pl.ds(half + part, part), :] = grams_sum[pl.ds(half, part), :] + over_x()
    over_z = exchange("z", lambda step: grams_sum.at[pl.ds(half + part, part)], grams_z)

    def total_rows(y, other_core=False):
        core = 1 - place.core if other_core else place.core
        start = core * half + lax.rem(place.y + y + SIDE, SIDE) * part
        return total_ref.at[pl.ds(pl.multiple_of(start, 8), part)]

    back_y = [mail.number() for _ in range(1, SIDE)]
    back_core = [mail.number() for _ in range(SIDE)]
    rings_y.first_ring()
    ring_y.near()
    start = place.core * half + place.y * part
    total_ref[pl.ds(pl.multiple_of(start, 8), part), :] = grams_sum[pl.ds(half + part, part), :] + over_z()
    for step in range(1, SIDE):
        mail.send(back_y[step - 1], total_rows(0), total_rows(0), place.at(y=step))
    mail.send(back_core[0], total_rows(0), total_rows(0), partner)
    rings_y.second_ring(0)
    rings_y.first_ring_far()
    ring_y.far()
    rings_y.second_ring(-1)
    for step in range(1, SIDE):
        mail.receive(back_y[step - 1], total_rows(-step), place.at(y=-step))
        mail.send(back_core[step], total_rows(-step), total_rows(-step), partner)
    rings_y.second_ring(1)
    rings_y.second_ring(2)
    for step in range(SIDE):
        mail.receive(back_core[step], total_rows(-step, True), partner)

    begin, step = coefficient_steps(panels, width, total_ref, v_own, of_y, of_v, of_w)

    def mix():
        mixing[...] = jnp.zeros_like(mixing)
        of_d, of_c = of_w[:, WIDE : 2 * WIDE], of_w[:, 2 * WIDE :]
        mixing[0:size, 0:WIDE] = of_d
        mixing[:, 0:WIDE] = mixing[:, 0:WIDE] + mixing[:, 0:WIDE].T
        mixing[0:size, WIDE:] = of_c

    def store_left(value, start, lane, low_lane):
        left = left_lanes((share, LANES))
        for at in range(2):
            top, rest = split(value[:, at * LANES : (at + 1) * LANES])
            if at:
                top = jnp.where(left, top, swap_halves(top))
                rest = jnp.where(left, rest, swap_halves(rest))
            here = pl.ds(start, share)
            low_here = slice(low_lane + at * LANES, low_lane + (at + 1) * LANES)
            left_low[here, low_here] = rest.astype(BF16)
            if not at:
                left_high[here, lane : lane + LANES] = top.astype(BF16)
            left_high[here, lane + (at + 1) * LANES : lane + (at + 2) * LANES] = top.astype(BF16)

    def left_rows(slot):
        unpack(row_y.at[slot], share_y, 0)
        here = pl.ds(slot * share, share)
        of_right_v = contract(row_wide[here, :], mixing[:, 0:WIDE], 1, 0, HIGH)
        of_right_v = of_right_v + contract(share_y[...], mixing[:, WIDE:], 1, 1, HIGH)
        of_right_y = contract(row_wide[here, :], mixing[:, WIDE:], 1, 0, HIGH)
        store_left(of_right_v, slot * share, 0, 0)
        store_left(of_right_y, slot * share, 3 * LANES, 2 * LANES)

    begin()
    step(0)
    step(1)
    step(2)
    step(3)
    step(4)
    step(5)
    mix()
    unpack(own, share_v, 0)
    unpack(share_sum, share_y, 0)
    w_ref[...] = contract(of_w[:, WIDE : 2 * WIDE], share_v[...], 1, 1, HIGH)
    w_ref[...] = w_ref[...] + contract(of_w[:, 2 * WIDE :], share_y[...], 1, 1, HIGH)
    ring_y.end()
    for slot in range(8):
        left_rows(slot)
    unpack_columns(col_y, 3 * LANES, NEAR)
    rings_y.last()
    unpack_columns(col_y, 3 * LANES, FAR)
    spread_v.finish()
    spread_y.finish()
    mail.finish()


def in_vmem(count):
    return [pl.BlockSpec(memory_space=pltpu.VMEM)] * count


def factors_call(v, matrix, panels, width):
    size, share = v.shape[0], v.shape[1] - width
    rows, lanes = share + share // 2, LANES
    height, length = matrix.shape
    grams = 4 * size
    part = grams // 8
    return pl.pallas_call(
        functools.partial(factors_kernel, panels, width),
        out_shape=(
            jax.ShapeDtypeStruct((length, 6 * lanes), BF16),
            jax.ShapeDtypeStruct((height, 6 * lanes), BF16),
            jax.ShapeDtypeStruct((height, 4 * lanes), BF16),
            jax.ShapeDtypeStruct((size, share), F32),
        ),
        in_specs=[pl.BlockSpec(memory_space=pltpu.HBM)] * 2,
        out_specs=in_vmem(4),
        scratch_shapes=[
            pltpu.VMEM((2, CHUNK, length), F32),
            pltpu.VMEM((height, length), BF16),
            pltpu.VMEM((height, length), BF16),
            pltpu.VMEM((8, rows, lanes), F32),
            pltpu.VMEM((8, rows, lanes), F32),
            pltpu.VMEM((16, rows, lanes), F32),
            pltpu.VMEM((16, rows, lanes), F32),
            pltpu.VMEM((height, WIDE), F32),
            pltpu.VMEM((size, height), F32),
            pltpu.VMEM((height, WIDE), F32),
            pltpu.VMEM((8, rows, lanes), F32),
            pltpu.VMEM((SIDE, rows, lanes), F32),
            pltpu.VMEM((SIDE, rows, lanes), F32),
            pltpu.VMEM((3, rows, lanes), F32),
            pltpu.VMEM((rows, lanes), F32),
            pltpu.VMEM((rows, lanes), F32),
            pltpu.VMEM(v.shape, F32),
            pltpu.VMEM((grams, lanes), F32),
            pltpu.VMEM((grams, lanes), F32),
            pltpu.VMEM((SIDE * part, lanes), F32),
            pltpu.VMEM((6 * part, lanes), F32),
            pltpu.VMEM((3, part, lanes), F32),
            pltpu.VMEM((3, part, lanes), F32),
            pltpu.VMEM((3, part, lanes), F32),
            pltpu.VMEM((size, 3 * WIDE), F32),
            pltpu.VMEM((size, 3 * WIDE), F32),
            pltpu.VMEM((size, 3 * WIDE), F32),
            pltpu.VMEM((WIDE, 2 * WIDE), F32),
            pltpu.VMEM((share, WIDE), F32),
            pltpu.VMEM((share, WIDE), F32),
            pltpu.SemaphoreType.DMA((192,)),
            pltpu.SemaphoreType.DMA((192,)),
            pltpu.SemaphoreType.DMA((5,)),
            pltpu.SemaphoreType.DMA((2,)),
        ],
        compiler_params=pltpu.CompilerParams(collective_id=0, has_side_effects=True, vmem_limit_bytes=35 * 1024 * 1024),
        cost_estimate=pl.CostEstimate(flops=50_000_000_000, bytes_accessed=100_000_000, transcendentals=0),
        name="factors",
    )(v, matrix)


TILE = 512


def update_kernel(matrix_ref, right_ref, high_ref, low_ref, w_in, out_ref, w_out):
    right = right_ref[...]
    change = contract(high_ref[...], right, 1, 1, None)
    low_v, low_y = low_ref[:, 0 : 2 * LANES], low_ref[:, 2 * LANES :]
    change = change + contract(low_v, right[:, LANES : 3 * LANES], 1, 1, None)
    change = change + contract(low_y, right[:, 4 * LANES :], 1, 1, None)
    out_ref[...] = matrix_ref[...] - change
    w_out[...] = w_in[...]


def update_call(matrix, right, left_high, left_low, w):
    height, length = matrix.shape

    return pl.pallas_call(
        update_kernel,
        grid=(length // TILE,),
        out_shape=(jax.ShapeDtypeStruct(matrix.shape, F32), jax.ShapeDtypeStruct(w.shape, F32)),
        in_specs=[
            pl.BlockSpec((height, TILE), lambda tile: (0, tile)),
            pl.BlockSpec((TILE, right.shape[1]), lambda tile: (tile, 0)),
            *in_vmem(3),
        ],
        out_specs=[pl.BlockSpec((height, TILE), lambda tile: (0, tile)), pl.BlockSpec(w.shape, lambda tile: (0, 0))],
        compiler_params=pltpu.CompilerParams(dimension_semantics=("arbitrary",), vmem_limit_bytes=22 * 1024 * 1024),
        name="update",
    )(matrix, right, left_high, left_low, w)


def per_device(trailing, v_panels, t_panels):
    panels, width, share = v_panels.shape
    size = panels * width
    v = jnp.concatenate([v_panels, t_panels], axis=2).reshape(size, share + width)
    right, left_high, left_low, w = factors_call(v, trailing, panels, width)
    matrix, w = update_call(trailing, right, left_high, left_low, w)
    return (matrix, w.reshape(panels, width, share))


def solution(mesh):
    return jax.shard_map(
        per_device,
        mesh=mesh,
        in_specs=(P("pr", "pc"), P(None, None, ("pr", "pc")), P()),
        out_specs=(P("pr", "pc"), P(None, None, ("pr", "pc"))),
        check_vma=False,
    )
```
